32 devices in a mesh: dp: 8 (over z, x), mp: 4 (over y, core).
Axes of the slice: x: 2, y: 2, z: 4, core: 2. Of those that a mesh axis runs over, the one named last changes fastest.
Arguments:
- table: float32 [25088, 512], P(('dp', 'mp')), may hold values from -6 to 6
- row_acc: float32 [25088], P(('dp', 'mp')), may hold values from 3.637979e-12 to 5.820766e-11
- uvqk_weight: float32 [512, 2048], replicated, may hold values from -0.25 to 0.25
- out_weight: float32 [512, 512], replicated, may hold values from -0.25 to 0.25
- time_bias: float32 [8, 32], replicated, may hold values from -0.6 to 0.6
- gains: float32 [3, 512], replicated, may hold values from 0.5 to 1.5
- uvqk_m: float32 [512, 2048], replicated, may hold values from -0.00032552084 to 0.00032552084
- uvqk_v: float32 [512, 2048], replicated, may hold values from 3.1370866e-09 to 5.0193385e-08
- out_m: float32 [512, 512], replicated, may hold values from -0.00032552084 to 0.00032552084
- out_v: float32 [512, 512], replicated, may hold values from 3.1370866e-09 to 5.0193385e-08
- bias_m: float32 [8, 32], replicated, may hold values from -0.00032552084 to 0.00032552084
- bias_v: float32 [8, 32], replicated, may hold values from 3.1370866e-09 to 5.0193385e-08
- gain_m: float32 [3, 512], replicated, may hold values from -0.00032552084 to 0.00032552084
- gain_v: float32 [3, 512], replicated, may hold values from 3.1370866e-09 to 5.0193385e-08
- lengths: int32 [32], P(('dp', 'mp')), may hold values from 1 to 1024, as said below
- time_buckets: int32 [32, 1024], P(('dp', 'mp')), may hold values from 0 to 31
- item_rows: int32 [49152], P(('dp', 'mp')), may hold values from 0 to 783
- row_owner: int32 [49152, 1], P(('dp', 'mp')), may hold values from 0 to 31; in each aligned block of 1536 rows (0 to 1535, 1536 to 3071, ...) at most 96 rows name the same one
Outputs:
- new_table: float32 [25088, 512], P(('dp', 'mp'))
- new_acc: float32 [25088], P(('dp', 'mp'))
- uvqk_step: float32 [512, 2048], replicated
- uvqk_m_new: float32 [512, 2048], replicated
- uvqk_v_new: float32 [512, 2048], replicated
- out_step: float32 [512, 512], replicated
- out_m_new: float32 [512, 512], replicated
- out_v_new: float32 [512, 512], replicated
- bias_step: float32 [8, 32], replicated
- bias_m_new: float32 [8, 32], replicated
- bias_v_new: float32 [8, 32], replicated
- gain_step: float32 [3, 512], replicated
- gain_m_new: float32 [3, 512], replicated
- gain_v_new: float32 [3, 512], replicated
- summary: float32 [3], replicated
- attention_rms: float32 [1], replicated
The draws below stay inside these ranges and needn't reach their ends.
Inputs may be any that keep to these rules, and one draw needn't show every extreme that they name: `lengths`: events of a history fill its first positions, the rest is padding. `row_owner`: among the 1536 requests of one device no owner is named more than 96 times.
All inputs are finite; a program needn't handle non-finite values.
Results may differ from the reference program's by a relative error of at most 0.0083.
Values may be sent and summed in bfloat16 or wider, within the bound.
No kernel may reach another device: no remote copies, remote signals or barrier semaphores. Data moves between devices by JAX's collectives and lax.ppermute only.
A program may use at most 128 MiB of HBM per device.

```python
import math
import jax
import jax.numpy as jnp
import numpy as np
from jax import lax

D = 512
H = 8
NB = 32
LEN = 1024
SEQ_DEV = 1
ROWS_DEV = 784
ITEMS = 25088
SEQS = 32
TOKENS = 32768
REQ_DEV = 1536
REQS = 49152
CAP = 96
N_DP = 8
N_MP = 4


def draw_lengths(key, part):
    seq_index = jnp.arange(SEQS, dtype=jnp.int32)
    upper_end = LEN // 3 + (LEN - LEN // 3) * (seq_index + 1) // SEQS
    lower_end = 2 * upper_end // 3
    offset = jax.random.randint(key, (SEQS,), 0, 1 << 20)
    drawn_len = lower_end + offset % (upper_end - lower_end + 1)
    return jnp.where(seq_index == SEQS - 1, LEN, drawn_len).astype(jnp.int32)


def touch_ends(values, key, least, top_value):
    spot = [jax.random.randint(jax.random.fold_in(key, axis), (), 0, length) for axis, length in enumerate(values.shape)]
    main_axis = values.shape.index(max(values.shape))
    neighbour = spot[:main_axis] + [(spot[main_axis] + 1) % values.shape[main_axis]] + spot[main_axis + 1:]
    return values.at[tuple(spot)].set(least).at[tuple(neighbour)].set(top_value)


def shard_levels(key, dims, pieces, low, top_value):
    def one(axis_at, shards_of):
        draws = jax.random.uniform(jax.random.fold_in(jax.random.fold_in(key, 6), axis_at), (shards_of,), jnp.float32, low / len(pieces), top_value / len(pieces))
        return jnp.repeat(jnp.exp(draws), dims[axis_at] // shards_of).reshape((-1,) + (1,) * (len(dims) - axis_at - 1))

    loudness = one(*pieces[0])
    for cut in pieces[1:]:
        loudness = loudness * one(*cut)
    return loudness


def shared_out(rng, own, number, rows, number_of, top, bound, lean):
    order = jax.random.permutation(rng, number_of)
    crowded, common = load_shares(number_of, rows * top, bound, lean, True), load_shares(number_of, rows * top, bound, lean, False)
    places = jnp.arange(number_of)

    def named(sizes, turn):
        used = int((sizes > 0).sum())
        fixed = max(1, used // 4)
        moved = fixed + (places - fixed + turn * (used - fixed)) % max(1, number_of - fixed)
        return jnp.zeros((number_of,), jnp.int32).at[order[jnp.where(places < fixed, places, moved)]].set(jnp.asarray(sizes, jnp.int32))

    sizes = jnp.where(number % 4 == 0, named(crowded, number // 4), named(common, number - number // 4 - 1))
    mixed = jax.random.permutation(jax.random.fold_in(own, 3), number_of)
    giver, receiver = mixed[0:number_of // 2 * 2:2], mixed[1:number_of // 2 * 2:2]
    room = jnp.minimum(sizes[giver] - 1, bound - sizes[receiver]) // 2
    room = jnp.where((giver == order[0]) | (receiver == order[0]) | (sizes[receiver] == 0), 0, jnp.maximum(room, 0))
    moved = jax.random.randint(jax.random.fold_in(own, 4), (number_of // 2,), 0, 1 << 20) % (room + 1)
    sizes = sizes.at[giver].add(-moved).at[receiver].add(moved)
    labels = jnp.searchsorted(jnp.cumsum(sizes), jnp.arange(rows * top), side="right").astype(jnp.int32)
    table = labels.reshape(top, rows).T
    table = table[jax.random.permutation(jax.random.fold_in(own, 1), rows)]
    turn = jax.random.randint(jax.random.fold_in(own, 2), (rows, 1), 0, top)
    return jnp.take_along_axis(table, (jnp.arange(top)[None, :] + turn) % top, axis=1)


def load_shares(number_of, total, bound, slope, full):
    portions = [(1 << 20) // math.isqrt(standing ** slope) + 1 for standing in range(1, number_of + 1)]
    largest = bound if full else min(bound, max(-(-total // number_of), total * portions[0] // sum(portions)))
    least = 1 if total - largest >= number_of - 1 else 0
    holding, rest = [largest] + [least] * (number_of - 1), total - largest - least * (number_of - 1)
    while rest > 0:
        candidates = [i for i in range(1, number_of) if holding[i] < largest] or [i for i in range(1, number_of) if holding[i] < bound]
        whole, left = sum([portions[i] for i in candidates]), rest
        for i in candidates:
            more = min(bound - holding[i], max(1, left * portions[i] // whole), rest)
            holding[i] = holding[i] + more
            rest = rest - more
    return np.array(holding)


def noise(rng, shape, deviation, most, pieces=(), kind=jnp.bfloat16):
    result = deviation * jax.random.normal(rng, shape, jnp.float32)
    if pieces:
        result = result * shard_levels(rng, shape, pieces, -0.22, 0.18)
    return jnp.clip(result, -most, most).astype(kind)


def setup_inputs(seed: int = 0) -> dict:
    keys = jax.random.split(jax.random.key(seed), 19)
    table = noise(keys[0], (ITEMS, D), 1.0, 6.0, ((0, 32),), jnp.float32)
    row_acc = jnp.clip(jnp.exp(math.log(5.820766091346741e-11) - 2.7725887 * jax.random.uniform(keys[1], (ITEMS,), jnp.float32) ** shard_levels(keys[1], (ITEMS,), ((0, 32),), -0.2, 0.2)), 3.637978807091713e-12, 5.820766091346741e-11)
    uvqk_weight = noise(keys[2], (D, 4 * D), D ** -0.5, 0.25, (), jnp.float32)
    out_weight = noise(keys[3], (D, D), D ** -0.5, 0.25, (), jnp.float32)
    time_bias = noise(keys[4], (H, NB), 0.1, 0.6, (), jnp.float32)
    gains = jnp.clip(1.0 + 0.1 * jax.random.normal(keys[5], (3, D), jnp.float32), 0.5, 1.5)
    uvqk_m = noise(keys[6], (D, 4 * D), (2.0 / (9 * (D * TOKENS) ** 0.5)), 0.00032552084, (), jnp.float32)
    uvqk_v = jnp.clip(jnp.exp(jax.random.uniform(keys[7], (D, 4 * D), jnp.float32, math.log(3.1370865904989387e-09), math.log(5.019338544798302e-08))), 3.1370865904989387e-09, 5.019338544798302e-08)
    out_m = noise(keys[8], (D, D), (2.0 / (9 * (D * TOKENS) ** 0.5)), 0.00032552084, (), jnp.float32)
    out_v = jnp.clip(jnp.exp(jax.random.uniform(keys[9], (D, D), jnp.float32, math.log(3.1370865904989387e-09), math.log(5.019338544798302e-08))), 3.1370865904989387e-09, 5.019338544798302e-08)
    bias_m = noise(keys[10], (H, NB), (2.0 / (9 * (D * TOKENS) ** 0.5)), 0.00032552084, (), jnp.float32)
    bias_v = jnp.clip(jnp.exp(jax.random.uniform(keys[11], (H, NB), jnp.float32, math.log(3.1370865904989387e-09), math.log(5.019338544798302e-08))), 3.1370865904989387e-09, 5.019338544798302e-08)
    gain_m = noise(keys[12], (3, D), (2.0 / (9 * (D * TOKENS) ** 0.5)), 0.00032552084, (), jnp.float32)
    gain_v = jnp.clip(jnp.exp(jax.random.uniform(keys[13], (3, D), jnp.float32, math.log(3.1370865904989387e-09), math.log(5.019338544798302e-08))), 3.1370865904989387e-09, 5.019338544798302e-08)
    lengths = draw_lengths(jax.random.fold_in(keys[18], 71), 0)
    time_buckets = touch_ends(jax.random.randint(keys[15], (SEQS, LEN), 0, NB), jax.random.fold_in(keys[15], 1), 0, NB - 1).astype(jnp.int32)
    item_rows = touch_ends(jax.random.randint(keys[16], (REQS,), 0, ROWS_DEV), jax.random.fold_in(keys[16], 1), 0, ROWS_DEV - 1).astype(jnp.int32)
    row_owner_keys = jax.random.split(jax.random.fold_in(keys[17], 1), REQS // REQ_DEV)
    row_owner_turns = jax.random.permutation(jax.random.fold_in(keys[17], 3), REQS // REQ_DEV)
    row_owner = jax.vmap(lambda own, number: shared_out(jax.random.fold_in(keys[17], 2), own, number, REQ_DEV, N_DP * N_MP, 1, CAP, 1))(row_owner_keys, row_owner_turns).reshape((REQS, 1))
    return {"table": table, "row_acc": row_acc, "uvqk_weight": uvqk_weight, "out_weight": out_weight, "time_bias": time_bias, "gains": gains, "uvqk_m": uvqk_m, "uvqk_v": uvqk_v, "out_m": out_m, "out_v": out_v, "bias_m": bias_m, "bias_v": bias_v, "gain_m": gain_m, "gain_v": gain_v, "lengths": lengths, "time_buckets": time_buckets, "item_rows": item_rows, "row_owner": row_owner}


EPSILON = 1e-06
ROW_RATE = 0.2
LEARN_RATE = 0.01
BETA_ONE = 0.9
BETA_TWO = 0.95
ADAM_EPSILON = 1e-08
WEIGHT_DECAY = 0.1
HIGHEST = lax.Precision.HIGHEST

@jax.custom_vjp
def low(v):
    return lax.optimization_barrier(v.astype(jnp.bfloat16)).astype(jnp.float32)

@jax.custom_vjp
def low_back(v):
    return v

def low_keep(v):
    return (low(v), None)

def low_pass(kept, grad):
    return (grad,)

def back_keep(v):
    return (v, None)

def back_low(kept, grad):
    return (low(grad),)
low.defvjp(low_keep, low_pass)
low_back.defvjp(back_keep, back_low)

def root_mean(values):
    return jnp.sqrt(lax.optimization_barrier(jnp.mean(values * values, -1)) + EPSILON)

def device_layer(w_uvqk, w_out, bias_in, gains_in, token_rows, neg_rows, seq_lens, buckets):
    seq_count, seq_len, model_width = token_rows.shape
    head_dim = model_width // H
    flat_rows = token_rows.reshape(-1, model_width)
    recip_one = lax.rsqrt(lax.optimization_barrier(jnp.mean(flat_rows * flat_rows, -1, keepdims=True)) + EPSILON)
    normed = low(flat_rows * recip_one * gains_in[0])
    project = low_back(jnp.dot(normed, w_uvqk, precision=HIGHEST))
    active = jax.nn.silu(project)
    gate_u = active[:, :model_width]
    value_qk = low(active[:, model_width:])
    value4 = value_qk[:, :model_width].reshape(seq_count, seq_len, H, head_dim)
    query4 = value_qk[:, model_width:2 * model_width].reshape(seq_count, seq_len, H, head_dim)
    key4 = value_qk[:, 2 * model_width:].reshape(seq_count, seq_len, H, head_dim)
    key_bias = jnp.transpose(bias_in[:, buckets], (1, 0, 2))
    raw_scores = jnp.einsum('sqhd,skhd->shqk', query4, key4, precision=HIGHEST)
    scores = low_back(raw_scores * head_dim ** (-0.5) + key_bias[:, :, None, :])
    positions = jnp.arange(seq_len, dtype=jnp.int32)
    keep_mask = (positions[None, None, :] <= positions[None, :, None]) & (positions[None, None, :] < seq_lens[:, None, None])
    weight = jnp.where(keep_mask, 1.0, 0.0).astype(jnp.float32) / seq_lens[:, None, None].astype(jnp.float32)
    attn = low(jax.nn.silu(scores) * weight[:, None])
    attended = low_back(jnp.einsum('shqk,skhd->sqhd', attn, value4, precision=HIGHEST).reshape(-1, model_width))
    recip_two = lax.rsqrt(lax.optimization_barrier(jnp.mean(attended * attended, -1, keepdims=True)) + EPSILON)
    gated = low(attended * recip_two * gains_in[1] * gate_u)
    branch = low_back(jnp.dot(gated, w_out, precision=HIGHEST))
    mixed = flat_rows + branch
    recip_three = lax.rsqrt(lax.optimization_barrier(jnp.mean(mixed * mixed, -1, keepdims=True)) + EPSILON)
    final = low(mixed * recip_three * gains_in[2])
    next_rows = jnp.concatenate([token_rows[:, 1:], jnp.zeros((seq_count, 1, model_width), jnp.float32)], 1).reshape(-1, model_width)
    logit_scale = 2.0 / math.sqrt(model_width)
    target = lax.optimization_barrier(jnp.sum(final * next_rows, -1)) * logit_scale
    negative = low_back(logit_scale * jnp.dot(final, neg_rows.T, precision=HIGHEST))
    top_logit = jnp.maximum(lax.optimization_barrier(jnp.max(negative, -1)), target)
    log_total = top_logit + jnp.log(jnp.exp(target - top_logit) + lax.optimization_barrier(jnp.sum(jnp.exp(negative - top_logit[:, None]), -1)))
    token_pos = jnp.tile(positions, seq_count)
    token_len = jnp.repeat(seq_lens, seq_len)
    loss_value = jnp.sum(jnp.where(token_pos < token_len - 1, log_total - target, 0.0))
    live_rows = token_pos < token_len
    statistics = jnp.stack([jnp.sum(jnp.where(live_rows, root_mean(flat_rows), 0.0)), jnp.sum(jnp.where(live_rows, root_mean(attended), 0.0)), jnp.sum(jnp.where(live_rows, root_mean(branch), 0.0))])
    return (loss_value, statistics)

def adam_update(weight, gradient, first, second, decay):
    first_new = BETA_ONE * first + (1.0 - BETA_ONE) * gradient
    second_new = BETA_TWO * second + (1.0 - BETA_TWO) * gradient * gradient
    update = -LEARN_RATE * (first_new / (jnp.sqrt(second_new) + ADAM_EPSILON) + decay * weight)
    return (update, first_new, second_new)

def reference(table, row_acc, uvqk_weight, out_weight, time_bias, gains, uvqk_m, uvqk_v, out_m, out_v, bias_m, bias_v, gain_m, gain_v, lengths, time_buckets, item_rows, row_owner):
    device_count = N_DP * N_MP
    flat_ids = (row_owner[:, 0] * ROWS_DEV + item_rows).astype(jnp.int32)

    def total_loss(table_in, w_uvqk, w_out, bias_in, gains_in):
        fetched = low(table_in[flat_ids]).reshape(device_count, REQ_DEV, D)
        token_rows = fetched[:, :SEQ_DEV * LEN].reshape(device_count, SEQ_DEV, LEN, D)
        neg_rows = fetched[:, SEQ_DEV * LEN:]
        low_uvqk = low(w_uvqk)
        low_out = low(w_out)

        def per_device(running, packed):
            loss_value, statistics = device_layer(low_uvqk, low_out, bias_in, gains_in, *packed)
            return ((running[0] + loss_value, running[1] + statistics), None)
        initial = (jnp.zeros((), jnp.float32), jnp.zeros((3,), jnp.float32))
        packs = (token_rows, neg_rows, lengths.reshape(device_count, SEQ_DEV), time_buckets.reshape(device_count, SEQ_DEV, LEN))
        (loss_value, statistics), _ = lax.scan(jax.checkpoint(per_device), initial, packs)
        return (loss_value / TOKENS, statistics / TOKENS)
    loss_value, pullback, statistics = jax.vjp(total_loss, table, uvqk_weight, out_weight, time_bias, gains, has_aux=True)
    grad_table, grad_uvqk, grad_out, grad_bias, grad_gains = pullback(jnp.ones((), jnp.float32))
    new_acc = row_acc + lax.optimization_barrier(jnp.mean(grad_table * grad_table, -1))
    new_table = table - ROW_RATE * grad_table * lax.rsqrt(new_acc)[:, None]
    uvqk_step, uvqk_m_new, uvqk_v_new = adam_update(uvqk_weight, grad_uvqk, uvqk_m, uvqk_v, WEIGHT_DECAY)
    out_step, out_m_new, out_v_new = adam_update(out_weight, grad_out, out_m, out_v, WEIGHT_DECAY)
    bias_step, bias_m_new, bias_v_new = adam_update(time_bias, grad_bias, bias_m, bias_v, 0.0)
    gain_step, gain_m_new, gain_v_new = adam_update(gains, grad_gains, gain_m, gain_v, 0.0)
    summary = jnp.stack([loss_value, statistics[0], statistics[2]])
    attention_rms = statistics[1:2]
    return (new_table, new_acc, uvqk_step, uvqk_m_new, uvqk_v_new, out_step, out_m_new, out_v_new, bias_step, bias_m_new, bias_v_new, gain_step, gain_m_new, gain_v_new, summary, attention_rms)
```

```python
import functools
import math

import jax
import jax.numpy as jnp
from jax import lax
from jax.experimental import pallas as pl
from jax.experimental.pallas import tpu as pltpu
from jax.sharding import Mesh
from jax.sharding import PartitionSpec as P

D = 512
H = 8
NB = 32

EPSILON = 1e-06
ROW_RATE = 0.2
LEARN_RATE = 0.01
BETA_ONE = 0.9
BETA_TWO = 0.95
ADAM_EPSILON = 1e-08
WEIGHT_DECAY = 0.1

ALL = ("zh", "b", "y", "c")
HALF = ("b", "y", "c")
CHIPS = ("zh", "b", "y")
SWAP = [(0, 1), (1, 0)]
BLK = 256
F32 = jnp.float32
BF16 = jnp.bfloat16
HIGH = lax.Precision.HIGHEST
PARAMS = pltpu.CompilerParams(vmem_limit_bytes=60 * 1024 * 1024)
NT = (((1,), (1,)), ((), ()))
TN = (((0,), (0,)), ((), ()))


def dot(left, right):
    return jnp.dot(left, right, preferred_element_type=F32)


def dot_nt(left, right):
    return lax.dot_general(left, right, NT, preferred_element_type=F32)


def dot_tn(left, right):
    return lax.dot_general(left, right, TN, preferred_element_type=F32)


def iota(shape, dim):
    return lax.broadcasted_iota(jnp.int32, shape, dim)


def one_hot(mask):
    return jnp.where(mask, 1.0, 0.0).astype(BF16)


def at(block):
    return pl.ds(pl.multiple_of(block * BLK, BLK), BLK)


def root_mean(mean_square):
    return jnp.sqrt(mean_square + EPSILON)


def mean_last(values):
    return jnp.mean(values, -1, keepdims=True)


def sds(*shape, dtype=BF16):
    return jax.ShapeDtypeStruct(shape, dtype)


def adam_update(weight, gradient, first, second, decay):
    first_new = BETA_ONE * first + (1.0 - BETA_ONE) * gradient
    second_new = BETA_TWO * second + (1.0 - BETA_TWO) * gradient * gradient
    update = -LEARN_RATE * (first_new / (jnp.sqrt(second_new) + ADAM_EPSILON) + decay * weight)
    return (update, first_new, second_new)


def slots_kernel(devices, capacity, half_ref, ownc_ref, ownr_ref, rows_ref, slotc_ref, slotr_ref, ids_ref):
    requests = ownc_ref.shape[0]
    peers = devices // 2
    shift = half_ref[0] * peers
    relc = ownc_ref[...] - shift
    relc = jnp.where(relc < 0, relc + devices, relc)
    relr = ownr_ref[...] - shift
    relr = jnp.where(relr < 0, relr + devices, relr)
    lower = one_hot(iota((BLK, BLK), 0) > iota((BLK, BLK), 1))
    upper = one_hot(iota((BLK, BLK), 0) < iota((BLK, BLK), 1))
    run_c = jnp.zeros((1, devices), F32)
    run_r = jnp.zeros((devices, 1), F32)
    acc_hi = jnp.zeros((peers, 2 * capacity), F32)
    acc_lo = jnp.zeros((peers, 2 * capacity), F32)
    for block in range(requests // BLK):
        part = slice(block * BLK, (block + 1) * BLK)
        rc = relc[part]
        hits = jnp.where(rc == iota((BLK, devices), 1), 1.0, 0.0)
        before = dot(lower, hits.astype(BF16)) + run_c
        rank = jnp.sum(before * hits, 1, keepdims=True).astype(jnp.int32)
        run_c = run_c + jnp.sum(hits, 0, keepdims=True)
        slotc_ref[part, :] = rc * capacity + rank
        rr = relr[:, part]
        hits_r = jnp.where(rr == iota((devices, BLK), 0), 1.0, 0.0)
        before_r = dot(hits_r.astype(BF16), upper) + run_r
        rank_r = jnp.sum(before_r * hits_r, 0, keepdims=True).astype(jnp.int32)
        run_r = run_r + jnp.sum(hits_r, 1, keepdims=True)
        slotr_ref[:, part] = rr * capacity + rank_r
        far = rc >= peers
        where = one_hot(iota((BLK, 2 * capacity), 1) == rank + jnp.where(far, capacity, 0))
        near_peer = jnp.where(rr >= peers, rr - peers, rr)
        mine = near_peer == iota((peers, BLK), 0)
        rows = rows_ref[:, part]
        hi = rows // 32
        lo = rows - hi * 32
        acc_hi = acc_hi + dot(jnp.where(mine, hi.astype(F32), 0.0).astype(BF16), where)
        acc_lo = acc_lo + dot(jnp.where(mine, lo.astype(F32), 0.0).astype(BF16), where)
    ids_ref[...] = (acc_hi * 32.0 + acc_lo).astype(jnp.int32)


def request_slots(half, owners, item_rows, devices, capacity):
    requests = item_rows.shape[0]
    vmem = pl.BlockSpec(memory_space=pltpu.VMEM)
    return pl.pallas_call(
        functools.partial(slots_kernel, devices, capacity),
        out_shape=(
            sds(requests, 1, dtype=jnp.int32),
            sds(1, requests, dtype=jnp.int32),
            sds(devices // 2, 2 * capacity, dtype=jnp.int32),
        ),
        in_specs=[pl.BlockSpec(memory_space=pltpu.SMEM)] + [vmem] * 3,
        out_specs=[vmem] * 3,
        compiler_params=PARAMS,
        name="request_slots",
    )(half, owners.reshape(requests, 1), owners.reshape(1, requests), item_rows.reshape(1, requests))


def serve_kernel(ids_ref, table_ref, out_ref):
    rows = table_ref.shape[0]
    for block in range(out_ref.shape[0] // BLK):
        part = slice(block * BLK, (block + 1) * BLK)
        hits = one_hot(ids_ref[part, :] == iota((BLK, rows), 1))
        out_ref[part, :] = dot(hits, table_ref[...]).astype(BF16)


def serve(ids, table):
    return pl.pallas_call(
        serve_kernel,
        out_shape=sds(ids.shape[0], table.shape[1]),
        compiler_params=PARAMS,
        name="serve",
    )(ids, table)


def place_kernel(slotc_ref, got_ref, out_ref):
    slots = got_ref.shape[0]
    for block in range(out_ref.shape[0] // BLK):
        part = slice(block * BLK, (block + 1) * BLK)
        hits = one_hot(slotc_ref[part, :] == iota((BLK, slots), 1))
        out_ref[part, :] = dot(hits, got_ref[...]).astype(BF16)


def place(slotc, got):
    return pl.pallas_call(
        place_kernel,
        out_shape=sds(slotc.shape[0], got.shape[1]),
        compiler_params=PARAMS,
        name="place",
    )(slotc, got)


def forward_kernel(
    total_tokens,
    len_ref,
    own_ref,
    far_ref,
    slotc_ref,
    w_ref,
    wo_ref,
    gains_ref,
    tb_ref,
    bucket_ref,
    x_ref,
    n1_ref,
    v_ref,
    q_ref,
    k_ref,
    sp_ref,
    bias_ref,
    dpu_ref,
    do_ref,
    gm_ref,
    dneg_ref,
    dout_ref,
    stats_ref,
    dgain_ref,
    xs,
    neg,
    gate,
    gate_d,
    att,
    dnacc,
    dwo,
    carry,
):
    seq_len = n1_ref.shape[0]
    negs = dneg_ref.shape[0]
    slots = far_ref.shape[0]
    blocks = seq_len // BLK
    length = len_ref[0]
    inv_len = 1.0 / (jnp.zeros((1, 1), jnp.int32) + length).astype(F32)

    def fetch(block):
        hits = one_hot(slotc_ref[at(block), :] - slots == iota((BLK, slots), 1))
        return own_ref[at(block), :].astype(F32) + dot(hits, far_ref[...])

    buckets = jnp.where(bucket_ref[...] == iota((NB, seq_len), 0), 1.0, 0.0)
    bias_ref[...] = 0.5 * jnp.dot(tb_ref[...], buckets, precision=HIGH, preferred_element_type=F32)
    xs[pl.ds(seq_len, 8), :] = jnp.zeros((8, D), F32)

    def project(block, sum_x):
        x = fetch(block)
        xs[at(block), :] = x
        x_ref[at(block), :] = x.astype(BF16)
        mean_sq = mean_last(x * x)
        pos = block * BLK + iota((BLK, 1), 0)
        live = pos < length
        n1 = (x * lax.rsqrt(mean_sq + EPSILON) * gains_ref[0:1, :]).astype(BF16)
        n1_ref[at(block), :] = n1
        for part in range(4):
            half_pre = 0.5 * dot(n1, w_ref[:, part * D : (part + 1) * D])
            th = jnp.tanh(half_pre)
            act = half_pre + half_pre * th
            deriv = 0.5 * (1.0 + th) * (1.0 + half_pre * (1.0 - th))
            if part == 0:
                gate[at(block), :] = act
                gate_d[at(block), :] = deriv
            else:
                sp_ref[at(block), (part - 1) * D : part * D] = deriv.astype(BF16)
                low = act.astype(BF16)
                if part == 1:
                    v_ref[at(block), :] = jnp.where(live, low.astype(F32), 0.0).astype(BF16)
                elif part == 2:
                    q_ref[at(block), :] = (low.astype(F32) * (0.5 * (D // H) ** -0.5)).astype(BF16)
                else:
                    k_ref[at(block), :] = low
        return sum_x + jnp.sum(jnp.where(live, root_mean(mean_sq), 0.0), keepdims=True)

    sum_x = lax.fori_loop(0, blocks, project, jnp.zeros((1, 1), F32))
    for block in range(negs // BLK):
        neg[block * BLK : (block + 1) * BLK, :] = fetch(blocks + block).astype(BF16)

    lower = iota((BLK, BLK), 0) >= iota((BLK, BLK), 1)

    def attend(pair, _):
        lanes = pl.ds(pl.multiple_of(pair * 128, 128), 128)
        lane = iota((1, 128), 1)
        sides = [jnp.where(lane < 64, 1.0, 0.0).astype(BF16), jnp.where(lane < 64, 0.0, 1.0).astype(BF16)]
        keys = [k_ref[:, lanes] * side for side in sides]
        vals = [v_ref[:, lanes] * side for side in sides]
        bias = [bias_ref[pl.ds(2 * pair + hh, 1), :] for hh in range(2)]
        for qb in range(blocks):
            query = q_ref[qb * BLK : (qb + 1) * BLK, lanes]
            total = jnp.zeros((BLK, 128), F32)
            for hh in range(2):
                for kb in range(qb + 1):
                    span = slice(kb * BLK, (kb + 1) * BLK)
                    half_s = dot_nt(query, keys[hh][span]) + bias[hh][:, span]
                    score = half_s + half_s * jnp.tanh(half_s)
                    if kb == qb:
                        score = jnp.where(lower, score, 0.0)
                    total = total + dot(score.astype(BF16), vals[hh][span])
            att[qb * BLK : (qb + 1) * BLK, lanes] = total * inv_len
        return 0

    lax.fori_loop(0, H // 2, attend, 0)

    scale = 2.0 / math.sqrt(D)
    dnacc[...] = jnp.zeros_like(dnacc)
    dwo[...] = jnp.zeros_like(dwo)
    carry[...] = jnp.zeros_like(carry)
    first_row = iota((BLK, 1), 0) == 0
    last_row = iota((BLK, 1), 0) == BLK - 1

    def head(block, sums):
        sum_loss, sum_o, sum_b, dg1, dg2 = sums
        rows = at(block)
        x = xs[rows, :]
        pos = block * BLK + iota((BLK, 1), 0)
        live = pos < length
        valid = pos < length - 1
        o = att[rows, :]
        u = gate[rows, :]
        ms_o = mean_last(o * o)
        r2 = lax.rsqrt(ms_o + EPSILON)
        n2 = o * r2 * gains_ref[1:2, :]
        g = (n2 * u).astype(BF16)
        branch = dot(g, wo_ref[...])
        ms_b = mean_last(branch * branch)
        mixed = x + branch
        r3 = lax.rsqrt(mean_last(mixed * mixed) + EPSILON)
        final = (mixed * r3 * gains_ref[2:3, :]).astype(BF16)
        final_f = final.astype(F32)
        after = xs[pl.ds(pl.multiple_of(block * BLK + BLK, 8), 8), :][0:1, :]
        nxt = jnp.where(last_row, after, pltpu.roll(x, BLK - 1, 0))
        target = jnp.sum(final_f * nxt, -1, keepdims=True) * scale
        logits = dot_nt(final, neg[...]) * scale
        top = jnp.maximum(jnp.max(logits, -1, keepdims=True), target)
        lse = top + jnp.log(jnp.exp(target - top) + jnp.sum(jnp.exp(logits - top), -1, keepdims=True))
        weight = jnp.where(valid, 1.0 / total_tokens, 0.0)
        dt = weight * (jnp.exp(target - lse) - 1.0) * scale
        dz = (weight * jnp.exp(logits - lse)).astype(BF16)
        dfin = dt * nxt + scale * dot(dz, neg[...])
        dnacc[...] += dot_tn(dz, final)
        dnext = dt * final_f
        shifted = jnp.where(first_row, carry[0:1, :], pltpu.roll(dnext, 1, 0))
        carry[...] = jnp.broadcast_to(dnext[BLK - 1 : BLK, :], carry.shape)
        dg2 = dg2 + jnp.sum(dfin * mixed * r3, 0, keepdims=True)
        scaled = dfin * gains_ref[2:3, :]
        dy = r3 * scaled - mixed * (r3 * r3 * r3) * mean_last(scaled * mixed)
        gm_ref[rows, :] = dy + shifted
        db = dy.astype(BF16)
        dwo[...] += dot_tn(g, db)
        dg = dot_nt(db, wo_ref[...])
        dpu_ref[rows, :] = (dg * n2 * gate_d[rows, :]).astype(BF16)
        dn2 = dg * u
        dg1 = dg1 + jnp.sum(dn2 * o * r2, 0, keepdims=True)
        scaled2 = dn2 * gains_ref[1:2, :]
        do = r2 * scaled2 - o * (r2 * r2 * r2) * mean_last(scaled2 * o)
        do_ref[rows, :] = (do * inv_len).astype(BF16)
        return (
            sum_loss + jnp.sum(jnp.where(valid, lse - target, 0.0), keepdims=True),
            sum_o + jnp.sum(jnp.where(live, root_mean(ms_o), 0.0), keepdims=True),
            sum_b + jnp.sum(jnp.where(live, root_mean(ms_b), 0.0), keepdims=True),
            dg1,
            dg2,
        )

    zero = jnp.zeros((1, 1), F32)
    zrow = jnp.zeros((1, D), F32)
    sum_loss, sum_o, sum_b, dg1, dg2 = lax.fori_loop(0, blocks, head, (zero, zero, zero, zrow, zrow))
    dneg_ref[...] = (dnacc[...] * scale).astype(BF16)
    dout_ref[...] = dwo[...].astype(BF16)
    which = iota((8, 128), 0)
    stats = jnp.where(which == 0, sum_loss, 0.0) + jnp.where(which == 1, sum_x, 0.0)
    stats_ref[...] = stats + jnp.where(which == 2, sum_o, 0.0) + jnp.where(which == 3, sum_b, 0.0)
    row = iota((8, D), 0)
    dgain_ref[...] = jnp.where(row == 1, dg1, 0.0) + jnp.where(row == 2, dg2, 0.0)


def forward(length, own, far, slotc, w, wo, gains, time_bias, buckets, total_tokens):
    seq_len = buckets.shape[1]
    negs = slotc.shape[0] - seq_len
    vmem = pl.BlockSpec(memory_space=pltpu.VMEM)
    outs = (
        sds(seq_len, D),
        sds(seq_len, D),
        sds(seq_len, D),
        sds(seq_len, D),
        sds(seq_len, D),
        sds(seq_len, 3 * D),
        sds(H, seq_len, dtype=F32),
        sds(seq_len, D),
        sds(seq_len, D),
        sds(seq_len, D, dtype=F32),
        sds(negs, D),
        sds(D, D),
        sds(8, 128, dtype=F32),
        sds(8, D, dtype=F32),
    )
    return pl.pallas_call(
        functools.partial(forward_kernel, total_tokens),
        out_shape=outs,
        in_specs=[pl.BlockSpec(memory_space=pltpu.SMEM)] + [vmem] * 8,
        out_specs=[vmem] * len(outs),
        scratch_shapes=[
            pltpu.VMEM((seq_len + 8, D), F32),
            pltpu.VMEM((negs, D), BF16),
            pltpu.VMEM((seq_len, D), F32),
            pltpu.VMEM((seq_len, D), F32),
            pltpu.VMEM((seq_len, D), F32),
            pltpu.VMEM((negs, D), F32),
            pltpu.VMEM((D, D), F32),
            pltpu.VMEM((8, D), F32),
        ],
        compiler_params=PARAMS,
        name="forward",
    )(length, own, far, slotc, w, wo, gains, time_bias, buckets)


def backward_kernel(
    len_ref,
    x_ref,
    v_ref,
    q_ref,
    k_ref,
    sp_ref,
    bias_ref,
    dpu_ref,
    do_ref,
    gm_ref,
    dneg_ref,
    slotr_ref,
    w_ref,
    gains_ref,
    bucket_ref,
    far_ref,
    own_ref,
    dp_ref,
    dbias_ref,
    dgain_ref,
    qt,
    dt,
    kt,
    vt,
    dkb,
    rows_ref,
):
    seq_len = x_ref.shape[0]
    requests = slotr_ref.shape[1]
    slots = far_ref.shape[0]
    blocks = seq_len // BLK
    length = len_ref[0]
    lower = iota((BLK, BLK), 0) >= iota((BLK, BLK), 1)
    live = iota((seq_len, 1), 0) < length
    ones = jnp.where(iota((16, seq_len), 0) == 0, 1.0, 0.0).astype(BF16)

    def pair_step(pair, _):
        lanes = pl.ds(pl.multiple_of(pair * 128, 128), 128)
        lane = iota((1, 128), 1)
        sides = [jnp.where(lane < 64, 1.0, 0.0).astype(BF16), jnp.where(lane < 64, 0.0, 1.0).astype(BF16)]
        keys = [k_ref[:, lanes] * side for side in sides]
        vals = [v_ref[:, lanes] * side for side in sides]
        bias = [bias_ref[pl.ds(2 * pair + hh, 1), :] for hh in range(2)]
        queries = q_ref[:, lanes]
        grads = do_ref[:, lanes]
        qtr = queries.astype(F32).T.astype(BF16)
        dtr = grads.astype(F32).T.astype(BF16)
        for hh in range(2):
            qt[hh, 0:64, :] = qtr[hh * 64 : hh * 64 + 64, :]
            qt[hh, 64:80, :] = ones
            dt[hh] = dtr[hh * 64 : hh * 64 + 64, :]
        kt[...] = jnp.zeros_like(kt)
        vt[...] = jnp.zeros_like(vt)
        for qb in range(blocks):
            qs = slice(qb * BLK, (qb + 1) * BLK)
            dq = jnp.zeros((BLK, 128), F32)
            for hh in range(2):
                for kb in range(qb + 1):
                    span = slice(kb * BLK, (kb + 1) * BLK)
                    half_s = dot_nt(queries[qs], keys[hh][span]) + bias[hh][:, span]
                    th = jnp.tanh(half_s)
                    score = half_s + half_s * th
                    deriv = (0.5 + 0.5 * th) * (1.0 + half_s - half_s * th)
                    ds = dot_nt(grads[qs], vals[hh][span]) * deriv
                    if kb == qb:
                        score = jnp.where(lower, score, 0.0)
                        ds = jnp.where(lower, ds, 0.0)
                    ds = ds.astype(BF16)
                    dq = dq + dot(ds, keys[hh][span])
                    kt[hh, :, span] += dot(qt[hh, :, qs], ds)
                    vt[hh, :, span] += dot(dt[hh, :, qs], score.astype(BF16))
            head_scale = (D // H) ** -0.5
            dql = pl.ds(pl.multiple_of(D + pair * 128, 128), 128)
            dp_ref[qs, dql] = (dq * head_scale * sp_ref[qs, dql].astype(F32)).astype(BF16)
        dkl = pl.ds(pl.multiple_of(2 * D + pair * 128, 128), 128)
        dk = jnp.concatenate([kt[0, 0:64, :], kt[1, 0:64, :]], 0).T
        dv = jnp.concatenate([vt[0], vt[1]], 0).T
        dp_ref[:, dkl] = (dk * 2.0 * sp_ref[:, dkl].astype(F32)).astype(BF16)
        dp_ref[:, lanes] = (jnp.where(live, dv, 0.0) * sp_ref[:, lanes].astype(F32)).astype(BF16)
        for hh in range(2):
            dkb[pl.ds(2 * pair + hh, 1), :] = kt[hh, 64:65, :]
        return 0

    lax.fori_loop(0, H // 2, pair_step, 0)
    buckets = jnp.where(bucket_ref[...] == iota((NB, seq_len), 0), 1.0, 0.0)
    dbias_ref[...] = lax.dot_general(dkb[...], buckets, NT, precision=HIGH, preferred_element_type=F32)

    def tail(block, dg0):
        rows = at(block)
        x = x_ref[rows, :].astype(F32)
        r1 = lax.rsqrt(mean_last(x * x) + EPSILON)
        dn1 = dot_nt(dpu_ref[rows, :], w_ref[:, 0:D]) + dot_nt(dp_ref[rows, :], w_ref[:, D : 4 * D])
        dg0 = dg0 + jnp.sum(dn1 * x * r1, 0, keepdims=True)
        scaled = dn1 * gains_ref[0:1, :]
        dx = r1 * scaled - x * (r1 * r1 * r1) * mean_last(scaled * x) + gm_ref[rows, :]
        rows_ref[rows, :] = dx.astype(BF16)
        return dg0

    dg0 = lax.fori_loop(0, blocks, tail, jnp.zeros((1, D), F32))
    rows_ref[seq_len:requests, :] = dneg_ref[...]
    dgain_ref[...] = jnp.where(iota((8, D), 0) == 0, dg0, 0.0)

    def put(block, _):
        slot = block * BLK + iota((BLK, 1), 0)
        hits = one_hot(slotr_ref[...] - slots == slot)
        far_ref[at(block), :] = dot(hits, rows_ref[...]).astype(BF16)
        hits = one_hot(slotr_ref[...] == slot)
        own_ref[at(block), :] = dot(hits, rows_ref[...]).astype(BF16)
        return 0

    lax.fori_loop(0, slots // BLK, put, 0)


def backward(length, x, v, q, k, sp, bias, dpu, do, gm, dneg, slotr, w, gains, buckets, slots):
    seq_len = x.shape[0]
    vmem = pl.BlockSpec(memory_space=pltpu.VMEM)
    outs = (
        sds(slots, D),
        sds(slots, D),
        sds(seq_len, 3 * D),
        sds(H, NB, dtype=F32),
        sds(8, D, dtype=F32),
    )
    return pl.pallas_call(
        backward_kernel,
        out_shape=outs,
        in_specs=[pl.BlockSpec(memory_space=pltpu.SMEM)] + [vmem] * 14,
        out_specs=[vmem] * len(outs),
        scratch_shapes=[
            pltpu.VMEM((2, 80, seq_len), BF16),
            pltpu.VMEM((2, 64, seq_len), BF16),
            pltpu.VMEM((2, 80, seq_len), F32),
            pltpu.VMEM((2, 64, seq_len), F32),
            pltpu.VMEM((H, seq_len), F32),
            pltpu.VMEM((slotr.shape[1], D), BF16),
        ],
        compiler_params=PARAMS,
        name="backward",
    )(length, x, v, q, k, sp, bias, dpu, do, gm, dneg, slotr, w, gains, buckets)


def weight_kernel(n1_ref, dp_ref, out_ref):
    for part in range(dp_ref.shape[1] // D):
        columns = slice(part * D, (part + 1) * D)
        out_ref[columns, :] = dot_tn(n1_ref[...], dp_ref[:, columns]).astype(BF16)


def weight_grad(n1, dp):
    return pl.pallas_call(
        weight_kernel,
        out_shape=sds(dp.shape[1], D),
        compiler_params=PARAMS,
        name="weight_grad",
    )(n1, dp)


def gather_kernel(ids_ref, got_ref, out_ref):
    rows, slots = (out_ref.shape[0], got_ref.shape[0])
    hits = one_hot(ids_ref[...] == iota((rows, slots), 0))
    out_ref[...] = dot(hits, got_ref[...]).astype(BF16)


def row_sums(ids, got, rows):
    return pl.pallas_call(
        gather_kernel,
        out_shape=sds(rows, got.shape[1]),
        compiler_params=PARAMS,
        name="row_sums",
    )(ids, got)


def update_kernel(ids_ref, got_ref, far_ref, table_ref, acc_ref, table_out, acc_out):
    rows, slots = (table_ref.shape[0], got_ref.shape[0])
    hits = one_hot(ids_ref[...] == iota((rows, slots), 0))
    sums = dot(hits, got_ref[...]) + far_ref[...].astype(F32)
    acc = acc_ref[...] + mean_last(sums * sums)
    acc_out[...] = acc
    table_out[...] = table_ref[...] - ROW_RATE * sums * lax.rsqrt(acc)


def update_rows(ids, got, far, table, row_acc):
    rows = table.shape[0]
    new_table, new_acc = pl.pallas_call(
        update_kernel,
        out_shape=(sds(*table.shape, dtype=F32), sds(rows, 1, dtype=F32)),
        compiler_params=PARAMS,
        name="update_rows",
    )(ids, got, far, table, row_acc.reshape(rows, 1))
    return new_table, new_acc.reshape(rows)


def sum_dense(grad):
    rows, width = grad.shape
    core = lax.axis_index("c")
    half = rows // 2
    chips = lax.axis_size(CHIPS)
    keep = lax.dynamic_slice_in_dim(grad, core * half, half, 0)
    give = lax.dynamic_slice_in_dim(grad, (1 - core) * half, half, 0)
    pair = (keep.astype(F32) + lax.ppermute(give, "c", SWAP).astype(F32)).astype(BF16)
    parts = lax.all_to_all(pair.reshape(chips, half // chips, width), CHIPS, 0, 0, tiled=True)
    mine = jnp.sum(parts.astype(F32), 0).astype(BF16)
    spread = lax.all_to_all(jnp.broadcast_to(mine[None], parts.shape), CHIPS, 0, 0, tiled=True)
    whole = spread.reshape(half, width)
    other = lax.ppermute(whole, "c", SWAP)
    return jnp.where(core == 0, jnp.concatenate([whole, other], 0), jnp.concatenate([other, whole], 0))


def per_device(
    table,
    row_acc,
    uvqk_weight,
    out_weight,
    time_bias,
    gains,
    uvqk_m,
    uvqk_v,
    out_m,
    out_v,
    bias_m,
    bias_v,
    gain_m,
    gain_v,
    lengths,
    time_buckets,
    item_rows,
    row_owner,
):
    devices = lax.axis_size(ALL)
    peers = devices // 2
    requests = item_rows.shape[0]
    capacity = max(2, 2 * requests // devices)
    rows = table.shape[0]
    slots = peers * capacity
    total_tokens = float(time_buckets.size * devices)
    half = lax.axis_index("zh").reshape(1)

    table_low = table.astype(BF16)
    table_far = lax.ppermute(table_low, "zh", SWAP)
    slotc, slotr, ids = request_slots(half, row_owner, item_rows, devices, capacity)
    ids = lax.all_to_all(ids, HALF, 0, 0, tiled=True)
    ids_own = ids[:, :capacity]
    ids_far = ids[:, capacity:]

    def exchange(values):
        return lax.all_to_all(
            values.reshape(peers, capacity, D), HALF, 0, 0, tiled=True
        ).reshape(slots, D)

    got_own = exchange(serve(ids_own.reshape(slots, 1), table_low))
    got_far = exchange(serve(ids_far.reshape(slots, 1), table_far))
    own = place(slotc, got_own)

    w_low = uvqk_weight.astype(BF16)
    wo_low = out_weight.astype(BF16)
    (x, n1, v, q, k, sp, bias, dpu, do, gm, dneg, dout, stats, dgain) = forward(
        lengths, own, got_far, slotc, w_low, wo_low, gains, time_bias, time_buckets, total_tokens
    )
    early = jnp.concatenate([dout, weight_grad(n1, dpu)], 0)
    send_far, send_own, dp, dbias, dgain0 = backward(
        lengths, x, v, q, k, sp, bias, dpu, do, gm, dneg, slotr, w_low, gains, time_buckets, slots
    )
    back_far = exchange(send_far)
    sums_far = row_sums(ids_far.reshape(1, slots), back_far, rows)
    sums_far = lax.ppermute(sums_far, "zh", SWAP)
    back_own = exchange(send_own)
    new_table, new_acc = update_rows(ids_own.reshape(1, slots), back_own, sums_far, table, row_acc)

    sum_early = sum_dense(early)
    sum_late = sum_dense(weight_grad(n1, dp))
    small = jnp.concatenate(
        [
            dbias.reshape(-1),
            (dgain + dgain0)[:3].reshape(-1),
            stats[:4, 0],
            jnp.zeros((2048 - H * NB - 3 * D - 4,), F32),
        ]
    ).reshape(1, 8, 256)
    small = lax.all_to_all(jnp.broadcast_to(small, (devices, 8, 256)), ALL, 0, 0, tiled=True)
    small = jnp.sum(small, 0).reshape(-1)
    sum_bias = small[: H * NB].reshape(H, NB)
    sum_gains = small[H * NB : H * NB + 3 * D].reshape(3, D)
    sums = small[H * NB + 3 * D : H * NB + 3 * D + 4] / total_tokens
    summary = jnp.stack([sums[0], sums[1], sums[3]])
    attention_rms = sums[2:3]

    sum_out = sum_early[:D].astype(F32)
    sum_uvqk = jnp.concatenate(
        [sum_early[D:], sum_late[:D], sum_late[D : 2 * D], sum_late[2 * D :]], 1
    ).astype(F32)
    uvqk_step, uvqk_m_new, uvqk_v_new = adam_update(
        uvqk_weight, sum_uvqk, uvqk_m, uvqk_v, WEIGHT_DECAY
    )
    out_step, out_m_new, out_v_new = adam_update(out_weight, sum_out, out_m, out_v, WEIGHT_DECAY)
    bias_step, bias_m_new, bias_v_new = adam_update(time_bias, sum_bias, bias_m, bias_v, 0.0)
    gain_step, gain_m_new, gain_v_new = adam_update(gains, sum_gains, gain_m, gain_v, 0.0)
    return (
        new_table,
        new_acc,
        uvqk_step,
        uvqk_m_new,
        uvqk_v_new,
        out_step,
        out_m_new,
        out_v_new,
        bias_step,
        bias_m_new,
        bias_v_new,
        gain_step,
        gain_m_new,
        gain_v_new,
        summary,
        attention_rms,
    )


def solution(mesh):
    n_dp, n_mp = (mesh.shape["dp"], mesh.shape["mp"])
    fine = Mesh(mesh.devices.reshape(2, n_dp // 2, n_mp // 2, 2), ALL)
    split = P(ALL)
    whole = P()
    return jax.shard_map(
        per_device,
        mesh=fine,
        in_specs=(split, split) + (whole,) * 12 + (split,) * 4,
        out_specs=(split, split) + (whole,) * 14,
        check_vma=False,
    )
```

```python
import functools
import math

import jax
import jax.numpy as jnp
from jax import lax
from jax.experimental import pallas as pl
from jax.experimental.pallas import tpu as pltpu
from jax.sharding import Mesh
from jax.sharding import PartitionSpec as P


D = 512
H = 8
NB = 32

EPSILON = 1e-06
ROW_RATE = 0.2
LEARN_RATE = 0.01
BETA_ONE = 0.9
BETA_TWO = 0.95
ADAM_EPSILON = 1e-08
WEIGHT_DECAY = 0.1

SWAP = [(0, 1), (1, 0)]
BLK = 256
F32 = jnp.float32
BF16 = jnp.bfloat16
HIGH = lax.Precision.HIGHEST
PARAMS = pltpu.CompilerParams(vmem_limit_bytes=60 * 1024 * 1024)
NT = (((1,), (1,)), ((), ()))
TN = (((0,), (0,)), ((), ()))


def dot(left, right):
    return jnp.dot(left, right, preferred_element_type=F32)


def dot_nt(left, right):
    return lax.dot_general(left, right, NT, preferred_element_type=F32)


def dot_tn(left, right):
    return lax.dot_general(left, right, TN, preferred_element_type=F32)


def iota(shape, dim):
    return lax.broadcasted_iota(jnp.int32, shape, dim)


def one_hot(mask):
    return jnp.where(mask, 1.0, 0.0).astype(BF16)


def at(block):
    return pl.ds(pl.multiple_of(block * BLK, BLK), BLK)


def root_mean(mean_square):
    return jnp.sqrt(mean_square + EPSILON)


def mean_last(values):
    return jnp.mean(values, -1, keepdims=True)


def sds(*shape, dtype=BF16):
    return jax.ShapeDtypeStruct(shape, dtype)


def adam_update(weight, gradient, first, second, decay):
    first_new = BETA_ONE * first + (1.0 - BETA_ONE) * gradient
    second_new = BETA_TWO * second + (1.0 - BETA_TWO) * gradient * gradient
    update = -LEARN_RATE * (first_new / (jnp.sqrt(second_new) + ADAM_EPSILON) + decay * weight)
    return (update, first_new, second_new)


def slots_kernel(devices, capacity, half_ref, ownc_ref, ownr_ref, rows_ref, slotc_ref, slotr_ref, ids_ref):
    requests = ownc_ref.shape[0]
    peers = devices // 2
    shift = half_ref[0] * peers
    relc = ownc_ref[...] - shift
    relc = jnp.where(relc < 0, relc + devices, relc)
    relr = ownr_ref[...] - shift
    relr = jnp.where(relr < 0, relr + devices, relr)
    lower = one_hot(iota((BLK, BLK), 0) > iota((BLK, BLK), 1))
    upper = one_hot(iota((BLK, BLK), 0) < iota((BLK, BLK), 1))
    run_c = jnp.zeros((1, devices), F32)
    run_r = jnp.zeros((devices, 1), F32)
    acc_hi = jnp.zeros((peers, 2 * capacity), F32)
    acc_lo = jnp.zeros((peers, 2 * capacity), F32)
    for block in range(requests // BLK):
        part = slice(block * BLK, (block + 1) * BLK)
        rc = relc[part]
        hits = jnp.where(rc == iota((BLK, devices), 1), 1.0, 0.0)
        before = dot(lower, hits.astype(BF16)) + run_c
        rank = jnp.sum(before * hits, 1, keepdims=True).astype(jnp.int32)
        run_c = run_c + jnp.sum(hits, 0, keepdims=True)
        slotc_ref[part, :] = rc * capacity + rank
        rr = relr[:, part]
        hits_r = jnp.where(rr == iota((devices, BLK), 0), 1.0, 0.0)
        before_r = dot(hits_r.astype(BF16), upper) + run_r
        rank_r = jnp.sum(before_r * hits_r, 0, keepdims=True).astype(jnp.int32)
        run_r = run_r + jnp.sum(hits_r, 1, keepdims=True)
        slotr_ref[:, part] = rr * capacity + rank_r
        far = rc >= peers
        where = one_hot(iota((BLK, 2 * capacity), 1) == rank + jnp.where(far, capacity, 0))
        near_peer = jnp.where(rr >= peers, rr - peers, rr)
        mine = near_peer == iota((peers, BLK), 0)
        rows = rows_ref[:, part]
        hi = rows // 32
        lo = rows - hi * 32
        acc_hi = acc_hi + dot(jnp.where(mine, hi.astype(F32), 0.0).astype(BF16), where)
        acc_lo = acc_lo + dot(jnp.where(mine, lo.astype(F32), 0.0).astype(BF16), where)
    ids_ref[...] = (acc_hi * 32.0 + acc_lo).astype(jnp.int32)


def request_slots(half, owners, item_rows, devices, capacity):
    requests = item_rows.shape[0]
    vmem = pl.BlockSpec(memory_space=pltpu.VMEM)
    return pl.pallas_call(
        functools.partial(slots_kernel, devices, capacity),
        out_shape=(
            sds(requests, 1, dtype=jnp.int32),
            sds(1, requests, dtype=jnp.int32),
            sds(devices // 2, 2 * capacity, dtype=jnp.int32),
        ),
        in_specs=[pl.BlockSpec(memory_space=pltpu.SMEM)] + [vmem] * 3,
        out_specs=[vmem] * 3,
        compiler_params=PARAMS,
        name="request_slots",
    )(half, owners.reshape(requests, 1), owners.reshape(1, requests), item_rows.reshape(1, requests))


def serve_kernel(ids_ref, table_ref, out_ref):
    rows = table_ref.shape[0]
    for block in range(out_ref.shape[0] // BLK):
        part = slice(block * BLK, (block + 1) * BLK)
        hits = one_hot(ids_ref[part, :] == iota((BLK, rows), 1))
        out_ref[part, :] = dot(hits, table_ref[...]).astype(BF16)


def serve(ids, table):
    return pl.pallas_call(
        serve_kernel,
        out_shape=sds(ids.shape[0], table.shape[1]),
        compiler_params=PARAMS,
        name="serve",
    )(ids, table)


def place_kernel(slotc_ref, got_ref, out_ref):
    slots = got_ref.shape[0]
    for block in range(out_ref.shape[0] // BLK):
        part = slice(block * BLK, (block + 1) * BLK)
        hits = one_hot(slotc_ref[part, :] == iota((BLK, slots), 1))
        out_ref[part, :] = dot(hits, got_ref[...]).astype(BF16)


def place(slotc, got):
    return pl.pallas_call(
        place_kernel,
        out_shape=sds(slotc.shape[0], got.shape[1]),
        compiler_params=PARAMS,
        name="place",
    )(slotc, got)


def step_kernel(
    total_tokens,
    len_ref,
    own_ref,
    far_ref,
    slotc_ref,
    slotr_ref,
    w_ref,
    wo_ref,
    gains_ref,
    tb_ref,
    bucketr_ref,
    bucketc_ref,
    out_ref,
    rows_ref,
    n1_ref,
    dp_ref,
    dout_ref,
    dbias_ref,
    stats_ref,
    dgain_ref,
    xs,
    neg,
    gate,
    deriv_ref,
    att,
    v_ref,
    q_ref,
    k_ref,
    baug,
    do_ref,
    abuf,
    sbuf,
    dnacc,
    dwo,
    carry,
    qt,
    dt,
    kt,
    vt,
    dkb,
):
    seq_len = n1_ref.shape[0]
    requests = slotc_ref.shape[0]
    negs = requests - seq_len
    slots = far_ref.shape[0]
    blocks = seq_len // BLK
    length = len_ref[0]
    inv_len = 1.0 / (jnp.zeros((1, 1), jnp.int32) + length).astype(F32)

    def fetch(block):
        hits = one_hot(slotc_ref[at(block), :] - slots == iota((BLK, slots), 1))
        return own_ref[at(block), :].astype(F32) + dot(hits, far_ref[...])

    xs[pl.ds(seq_len, 8), :] = jnp.zeros((8, D), F32)
    tb = 0.5 * tb_ref[...]
    tb_hi = tb.astype(BF16)
    tb_lo = (tb - tb_hi.astype(F32)).astype(BF16)
    head = iota((H, D), 0)
    spot = head // 2 * 128 + jnp.where(head % 2 == 0, 64, 0)
    lane_of = iota((H, D), 1)
    terms = dot_tn(tb_hi, one_hot(lane_of == spot)) + dot_tn(tb_lo, one_hot(lane_of == spot + 1))
    terms = terms.astype(BF16)

    def project(block, sum_x):
        rows = at(block)
        x = fetch(block)
        xs[rows, :] = x
        baug[rows, :] = dot(one_hot(bucketc_ref[rows, :] == iota((BLK, NB), 1)), terms).astype(BF16)
        mean_sq = mean_last(x * x)
        pos = block * BLK + iota((BLK, 1), 0)
        live = pos < length
        n1 = (x * lax.rsqrt(mean_sq + EPSILON) * gains_ref[0:1, :]).astype(BF16)
        n1_ref[rows, :] = n1
        for part in range(4):
            half_pre = dot(n1, w_ref[:, part * D : (part + 1) * D])
            th = jnp.tanh(half_pre)
            bend = half_pre * th
            act = half_pre + bend
            deriv_ref[rows, part * D : (part + 1) * D] = ((1.0 + th) * (1.0 + half_pre - bend)).astype(BF16)
            if part == 0:
                gate[rows, :] = act
            elif part == 1:
                v_ref[rows, :] = jnp.where(live, act, 0.0).astype(BF16)
            elif part == 2:
                q_ref[rows, :] = (act * (0.5 * (D // H) ** -0.5)).astype(BF16)
            else:
                k_ref[rows, :] = act.astype(BF16)
        return sum_x + jnp.sum(jnp.where(live, root_mean(mean_sq), 0.0), keepdims=True)

    sum_x = lax.fori_loop(0, blocks, project, jnp.zeros((1, 1), F32))

    def fetch_neg(block, _):
        neg[at(block), :] = fetch(blocks + block).astype(BF16)
        return 0

    lax.fori_loop(0, negs // BLK, fetch_neg, 0)

    lower = iota((BLK, BLK), 0) >= iota((BLK, BLK), 1)
    lane = iota((1, 128), 1)
    sides = [one_hot(lane < 64), one_hot(lane >= 64)]
    marks = [one_hot(lane // 2 == 32), one_hot(lane // 2 == 0)]

    def attend(pair, _):
        lanes = pl.ds(pl.multiple_of(pair * 128, 128), 128)
        bias = baug[:, lanes]
        keys = [k_ref[:, lanes] * sides[hh] + bias * sides[1 - hh] for hh in range(2)]
        vals = [v_ref[:, lanes] * sides[hh] for hh in range(2)]
        for qb in range(blocks):
            qs = slice(qb * BLK, (qb + 1) * BLK)
            total = jnp.zeros((BLK, 128), F32)
            for hh in range(2):
                query = q_ref[qs, lanes] * sides[hh] + marks[hh]
                for kb in range(qb + 1):
                    span = slice(kb * BLK, (kb + 1) * BLK)
                    half_s = dot_nt(query, keys[hh][span])
                    th = jnp.tanh(half_s)
                    bend = half_s * th
                    score = half_s + bend
                    deriv = (1.0 + th) * (1.0 + half_s - bend)
                    if kb == qb:
                        score = jnp.where(lower, score, 0.0)
                        deriv = jnp.where(lower, deriv, 0.0)
                    low = score.astype(BF16)
                    tile = qb * (qb + 1) // 2 + kb
                    abuf[2 * pair + hh, tile] = low
                    sbuf[2 * pair + hh, tile] = deriv.astype(BF16)
                    total = total + dot(low, vals[hh][span])
            att[qs, lanes] = total * inv_len
        return 0

    lax.fori_loop(0, H // 2, attend, 0)

    scale = 2.0 / math.sqrt(D)
    dnacc[...] = jnp.zeros_like(dnacc)
    dwo[...] = jnp.zeros_like(dwo)
    carry[...] = jnp.zeros_like(carry)
    first_row = iota((BLK, 1), 0) == 0
    last_row = iota((BLK, 1), 0) == BLK - 1

    def middle(block, sums):
        sum_loss, sum_o, sum_b, dg1, dg2 = sums
        rows = at(block)
        x = xs[rows, :]
        pos = block * BLK + iota((BLK, 1), 0)
        live = pos < length
        valid = pos < length - 1
        o = att[rows, :]
        u = gate[rows, :]
        ms_o = mean_last(o * o)
        r2 = lax.rsqrt(ms_o + EPSILON)
        n2 = o * r2 * gains_ref[1:2, :]
        g = (n2 * u).astype(BF16)
        branch = dot(g, wo_ref[...])
        ms_b = mean_last(branch * branch)
        mixed = x + branch
        r3 = lax.rsqrt(mean_last(mixed * mixed) + EPSILON)
        final = (mixed * r3 * gains_ref[2:3, :]).astype(BF16)
        final_f = final.astype(F32)
        after = xs[pl.ds(pl.multiple_of(block * BLK + BLK, 8), 8), :][0:1, :]
        nxt = jnp.where(last_row, after, pltpu.roll(x, BLK - 1, 0))
        target = jnp.sum(final_f * nxt, -1, keepdims=True) * scale
        logits = dot_nt(final, neg[...]) * scale
        top = jnp.maximum(jnp.max(logits, -1, keepdims=True), target)
        powers = jnp.exp(logits - top)
        near = jnp.exp(target - top)
        total = near + jnp.sum(powers, -1, keepdims=True)
        lse = top + jnp.log(total)
        weight = jnp.where(valid, 1.0 / total_tokens, 0.0)
        share = weight / total
        dt_ = (share * near - weight) * scale
        dz = (share * powers).astype(BF16)
        dfin = dt_ * nxt + scale * dot(dz, neg[...])
        dnacc[...] += dot_tn(dz, final)
        dnext = dt_ * final_f
        shifted = jnp.where(first_row, carry[0:1, :], pltpu.roll(dnext, 1, 0))
        carry[...] = jnp.broadcast_to(dnext[BLK - 1 : BLK, :], carry.shape)
        unit3 = mixed * r3
        dg2 = dg2 + jnp.sum(dfin * unit3, 0, keepdims=True)
        scaled = dfin * gains_ref[2:3, :]
        dy = r3 * (scaled - unit3 * mean_last(scaled * unit3))
        att[rows, :] = dy + shifted
        db = dy.astype(BF16)
        dwo[...] += dot_tn(g, db)
        dg = dot_nt(db, wo_ref[...])
        dp_ref[rows, 0:D] = (0.5 * dg * n2 * deriv_ref[rows, 0:D].astype(F32)).astype(BF16)
        dn2 = dg * u
        unit2 = o * r2
        dg1 = dg1 + jnp.sum(dn2 * unit2, 0, keepdims=True)
        scaled2 = dn2 * gains_ref[1:2, :]
        do = (r2 * (0.5 * inv_len)) * (scaled2 - unit2 * mean_last(scaled2 * unit2))
        do_ref[rows, :] = do.astype(BF16)
        return (
            sum_loss + jnp.sum(jnp.where(valid, lse - target, 0.0), keepdims=True),
            sum_o + jnp.sum(jnp.where(live, root_mean(ms_o), 0.0), keepdims=True),
            sum_b + jnp.sum(jnp.where(live, root_mean(ms_b), 0.0), keepdims=True),
            dg1,
            dg2,
        )

    zero = jnp.zeros((1, 1), F32)
    zrow = jnp.zeros((1, D), F32)
    sum_loss, sum_o, sum_b, dg1, dg2 = lax.fori_loop(0, blocks, middle, (zero, zero, zero, zrow, zrow))
    rows_ref[seq_len:requests, :] = (dnacc[...] * scale).astype(BF16)
    dout_ref[...] = dwo[...].astype(BF16)
    which = iota((8, 128), 0)
    stats = jnp.where(which == 0, sum_loss, 0.0) + jnp.where(which == 1, sum_x, 0.0)
    stats_ref[...] = stats + jnp.where(which == 2, sum_o, 0.0) + jnp.where(which == 3, sum_b, 0.0)

    ones = one_hot(iota((16, seq_len), 0) == 0)
    alive = iota((seq_len, 1), 0) < length

    def attend_back(pair, _):
        lanes = pl.ds(pl.multiple_of(pair * 128, 128), 128)
        keys = [k_ref[:, lanes] * side for side in sides]
        vals = [v_ref[:, lanes] * side for side in sides]
        grads = do_ref[:, lanes]
        qtr = q_ref[:, lanes].astype(F32).T.astype(BF16)
        dtr = grads.astype(F32).T.astype(BF16)
        for hh in range(2):
            qt[hh, 0:64, :] = qtr[hh * 64 : hh * 64 + 64, :]
            qt[hh, 64:80, :] = ones
            dt[hh] = dtr[hh * 64 : hh * 64 + 64, :]
        kt[...] = jnp.zeros_like(kt)
        vt[...] = jnp.zeros_like(vt)
        dql = pl.ds(pl.multiple_of(2 * D + pair * 128, 128), 128)
        for qb in range(blocks):
            qs = slice(qb * BLK, (qb + 1) * BLK)
            dq = jnp.zeros((BLK, 128), F32)
            for hh in range(2):
                for kb in range(qb + 1):
                    span = slice(kb * BLK, (kb + 1) * BLK)
                    tile = qb * (qb + 1) // 2 + kb
                    slope = sbuf[2 * pair + hh, tile].astype(F32)
                    ds = (dot_nt(grads[qs], vals[hh][span]) * slope).astype(BF16)
                    dq = dq + dot(ds, keys[hh][span])
                    kt[hh, :, span] += dot(qt[hh, :, qs], ds)
                    vt[hh, :, span] += dot(dt[hh, :, qs], abuf[2 * pair + hh, tile])
            dq = dq * (0.5 * (D // H) ** -0.5)
            dp_ref[qs, dql] = (dq * deriv_ref[qs, dql].astype(F32)).astype(BF16)
        dkl = pl.ds(pl.multiple_of(3 * D + pair * 128, 128), 128)
        dvl = pl.ds(pl.multiple_of(D + pair * 128, 128), 128)
        dk = jnp.concatenate([kt[0, 0:64, :], kt[1, 0:64, :]], 0).T
        dv = jnp.concatenate([vt[0], vt[1]], 0).T
        dp_ref[:, dkl] = (dk * deriv_ref[:, dkl].astype(F32)).astype(BF16)
        dp_ref[:, dvl] = (jnp.where(alive, dv, 0.0) * deriv_ref[:, dvl].astype(F32)).astype(BF16)
        for hh in range(2):
            dkb[pl.ds(2 * pair + hh, 1), :] = kt[hh, 64:65, :]
        return 0

    lax.fori_loop(0, H // 2, attend_back, 0)
    buckets = jnp.where(bucketr_ref[...] == iota((NB, seq_len), 0), 1.0, 0.0)
    dbias_ref[...] = lax.dot_general(dkb[...], buckets, NT, precision=HIGH, preferred_element_type=F32)

    def tail(block, dg0):
        rows = at(block)
        x = xs[rows, :]
        r1 = lax.rsqrt(mean_last(x * x) + EPSILON)
        unit1 = x * r1
        dn1 = dot_nt(dp_ref[rows, :], w_ref[...])
        dg0 = dg0 + jnp.sum(dn1 * unit1, 0, keepdims=True)
        scaled = dn1 * (2.0 * gains_ref[0:1, :])
        dx = r1 * (scaled - unit1 * mean_last(scaled * unit1)) + att[rows, :]
        rows_ref[rows, :] = dx.astype(BF16)
        return dg0

    dg0 = 2.0 * lax.fori_loop(0, blocks, tail, zrow)
    row = iota((8, D), 0)
    gsum = jnp.where(row == 0, dg0, 0.0) + jnp.where(row == 1, dg1, 0.0)
    dgain_ref[...] = gsum + jnp.where(row == 2, dg2, 0.0)

    def put(block, _):
        slot = slots + block * BLK + iota((BLK, 1), 0)
        out_ref[at(block), :] = dot(one_hot(slotr_ref[...] == slot), rows_ref[...]).astype(BF16)
        return 0

    lax.fori_loop(0, slots // BLK, put, 0)


def step(length, own, far, slotc, slotr, w, wo, gains, time_bias, buckets, total_tokens):
    seq_len = buckets.shape[1]
    requests = slotc.shape[0]
    negs = requests - seq_len
    slots = far.shape[0]
    vmem = pl.BlockSpec(memory_space=pltpu.VMEM)
    blocks = seq_len // BLK
    tiles = blocks * (blocks + 1) // 2
    outs = (
        sds(slots, D),
        sds(requests, D),
        sds(seq_len, D),
        sds(seq_len, 4 * D),
        sds(D, D),
        sds(H, NB, dtype=F32),
        sds(8, 128, dtype=F32),
        sds(8, D, dtype=F32),
    )
    return pl.pallas_call(
        functools.partial(step_kernel, total_tokens),
        out_shape=outs,
        in_specs=[pl.BlockSpec(memory_space=pltpu.SMEM)] + [vmem] * 10,
        out_specs=[vmem] * len(outs),
        scratch_shapes=[
            pltpu.VMEM((seq_len + 8, D), F32),
            pltpu.VMEM((negs, D), BF16),
            pltpu.VMEM((seq_len, D), F32),
            pltpu.VMEM((seq_len, 4 * D), BF16),
            pltpu.VMEM((seq_len, D), F32),
            pltpu.VMEM((seq_len, D), BF16),
            pltpu.VMEM((seq_len, D), BF16),
            pltpu.VMEM((seq_len, D), BF16),
            pltpu.VMEM((seq_len, D), BF16),
            pltpu.VMEM((seq_len, D), BF16),
            pltpu.VMEM((H, tiles, BLK, BLK), BF16),
            pltpu.VMEM((H, tiles, BLK, BLK), BF16),
            pltpu.VMEM((negs, D), F32),
            pltpu.VMEM((D, D), F32),
            pltpu.VMEM((8, D), F32),
            pltpu.VMEM((2, 80, seq_len), BF16),
            pltpu.VMEM((2, 64, seq_len), BF16),
            pltpu.VMEM((2, 80, seq_len), F32),
            pltpu.VMEM((2, 64, seq_len), F32),
            pltpu.VMEM((H, seq_len), F32),
        ],
        compiler_params=PARAMS,
        cost_estimate=pl.CostEstimate(flops=50_000_000_000, bytes_accessed=15_000_000, transcendentals=0),
        name="step",
    )(length, own, far, slotc, slotr, w, wo, gains, time_bias, buckets, buckets.reshape(seq_len, 1))


def spread_kernel(slotr_ref, rows_ref, out_ref):
    def put(block, _):
        slot = block * BLK + iota((BLK, 1), 0)
        out_ref[at(block), :] = dot(one_hot(slotr_ref[...] == slot), rows_ref[...]).astype(BF16)
        return 0

    lax.fori_loop(0, out_ref.shape[0] // BLK, put, 0)


def spread(slotr, rows, slots):
    return pl.pallas_call(
        spread_kernel,
        out_shape=sds(slots, D),
        compiler_params=PARAMS,
        name="spread",
    )(slotr, rows)


def weight_kernel(n1_ref, dp_ref, out_ref, turned):
    @pl.when(pl.program_id(0) == 0)
    def _():
        turned[...] = n1_ref[...].astype(F32).T.astype(BF16)

    out_ref[...] = dot(turned[...], dp_ref[...]).astype(BF16)


def weight_grad(n1, dp):
    parts = dp.shape[1] // D
    seq_len = n1.shape[0]
    return pl.pallas_call(
        weight_kernel,
        grid=(parts,),
        out_shape=sds(dp.shape[1], D),
        in_specs=[pl.BlockSpec((seq_len, D), lambda i: (0, 0)), pl.BlockSpec((seq_len, D), lambda i: (0, i))],
        out_specs=pl.BlockSpec((D, D), lambda i: (i, 0)),
        scratch_shapes=[pltpu.VMEM((D, seq_len), BF16)],
        compiler_params=PARAMS,
        name="weight_grad",
    )(n1, dp)


def gather_kernel(ids_ref, got_ref, out_ref):
    rows, slots = (out_ref.shape[0], got_ref.shape[0])
    hits = one_hot(ids_ref[...] == iota((rows, slots), 0))
    out_ref[...] = dot(hits, got_ref[...]).astype(BF16)


def row_sums(ids, got, rows):
    return pl.pallas_call(
        gather_kernel,
        out_shape=sds(rows, got.shape[1]),
        compiler_params=PARAMS,
        name="row_sums",
    )(ids, got)


def update_kernel(ids_ref, got_ref, far_ref, table_ref, acc_ref, table_out, acc_out):
    rows, slots = (table_ref.shape[0], got_ref.shape[0])
    hits = one_hot(ids_ref[...] == iota((rows, slots), 0))
    sums = dot(hits, got_ref[...]) + far_ref[...].astype(F32)
    acc = acc_ref[...] + mean_last(sums * sums)
    acc_out[...] = acc
    table_out[...] = table_ref[...] - ROW_RATE * sums * lax.rsqrt(acc)


def update_rows(ids, got, far, table, row_acc):
    rows = table.shape[0]
    new_table, new_acc = pl.pallas_call(
        update_kernel,
        out_shape=(sds(*table.shape, dtype=F32), sds(rows, 1, dtype=F32)),
        compiler_params=PARAMS,
        name="update_rows",
    )(ids, got, far, table, row_acc.reshape(rows, 1))
    return new_table, new_acc.reshape(rows)


def sum_chips(grad, axes):
    pair = axes[-1]
    chips = axes[:-1]
    rows, width = grad.shape
    core = lax.axis_index(pair)
    half = rows // 2
    keep = lax.dynamic_slice_in_dim(grad, core * half, half, 0)
    give = lax.dynamic_slice_in_dim(grad, (1 - core) * half, half, 0)
    part = keep.astype(F32) + lax.ppermute(give, pair, SWAP).astype(F32)
    part = part.astype(BF16).reshape((2,) * len(chips) + (half >> len(chips), width))
    for dim in reversed(range(len(chips))):
        here = lax.axis_index(chips[dim])
        give = lax.dynamic_index_in_dim(part, 1 - here, dim, keepdims=True)
        keep = lax.dynamic_index_in_dim(part, here, dim, keepdims=True)
        got = lax.ppermute(give, chips[dim], SWAP)
        part = (keep.astype(F32) + got.astype(F32)).astype(BF16)
    return part.reshape(half >> len(chips), width)


def share_chips(part, extra, axes):
    pair = axes[-1]
    chips = axes[:-1]
    count = lax.axis_size(chips)
    rows, width = part.shape
    packed = jnp.concatenate([part, extra], 0)[None]
    got = lax.all_to_all(jnp.broadcast_to(packed, (count,) + packed.shape[1:]), chips, 0, 0, tiled=True)
    whole = got[:, :rows].reshape(count * rows, width)
    other = lax.ppermute(whole, pair, SWAP)
    core = lax.axis_index(pair)
    dense = jnp.where(core == 0, jnp.concatenate([whole, other], 0), jnp.concatenate([other, whole], 0))
    return dense, got[:, rows:]


def per_device(
    axes,
    table,
    row_acc,
    uvqk_weight,
    out_weight,
    time_bias,
    gains,
    uvqk_m,
    uvqk_v,
    out_m,
    out_v,
    bias_m,
    bias_v,
    gain_m,
    gain_v,
    lengths,
    time_buckets,
    item_rows,
    row_owner,
):
    every = axes
    near = axes[1:]
    devices = lax.axis_size(every)
    peers = devices // 2
    requests = item_rows.shape[0]
    capacity = max(2, 2 * requests // devices)
    rows = table.shape[0]
    slots = peers * capacity
    total_tokens = float(time_buckets.size * devices)
    half = lax.axis_index(axes[0]).reshape(1)

    def exchange(values):
        return lax.all_to_all(values.reshape(peers, capacity, D), near, 0, 0, tiled=True).reshape(slots, D)

    table_low = table.astype(BF16)
    table_far = lax.ppermute(table_low, axes[0], SWAP)
    slotc, slotr, ids = request_slots(half, row_owner, item_rows, devices, capacity)
    ids = lax.all_to_all(ids, near, 0, 0, tiled=True)
    ids_own = ids[:, :capacity]
    ids_far = ids[:, capacity:]
    serve_own = serve(ids_own.reshape(slots, 1), table_low)
    got_own = exchange(serve_own)
    serve_far = serve(ids_far.reshape(slots, 1), table_far)
    got_far = exchange(serve_far)
    own = place(slotc, got_own)

    w_low = (0.5 * uvqk_weight).astype(BF16)
    wo_low = out_weight.astype(BF16)
    send_far, row_grads, n1, dp, dout, dbias, stats, dgain = step(
        lengths, own, got_far, slotc, slotr, w_low, wo_low, gains, time_bias, time_buckets, total_tokens
    )
    back_far = exchange(send_far)
    send_own = spread(slotr, row_grads, slots)
    dense = jnp.concatenate([dout, weight_grad(n1, dp)], 0)
    sums_far = row_sums(ids_far.reshape(1, slots), back_far, rows)
    sums_far = lax.ppermute(sums_far, axes[0], SWAP)
    back_own = exchange(send_own)
    new_table, new_acc = update_rows(ids_own.reshape(1, slots), back_own, sums_far, table, row_acc)

    small = jnp.concatenate(
        [
            dbias.reshape(-1),
            dgain[:3].reshape(-1),
            stats[:4, 0],
            jnp.zeros((2048 - H * NB - 3 * D - 4,), F32),
        ]
    ).reshape(4, D)
    small = small + lax.ppermute(small, axes[-1], SWAP)
    small_hi = lax.reduce_precision(small, 8, 7)
    small_lo = (small - small_hi).astype(BF16)
    small_hi = small_hi.astype(BF16)
    part = sum_chips(dense, axes)
    dense, small = share_chips(part, jnp.concatenate([small_hi, small_lo], 0), axes)
    small = jnp.sum(small.astype(F32), 0)
    small = (small[:4] + small[4:]).reshape(-1)
    sum_bias = small[: H * NB].reshape(H, NB)
    sum_gains = small[H * NB : H * NB + 3 * D].reshape(3, D)
    sums = small[H * NB + 3 * D : H * NB + 3 * D + 4] / total_tokens
    summary = jnp.stack([sums[0], sums[1], sums[3]])
    attention_rms = sums[2:3]

    sum_out = dense[:D].astype(F32)
    sum_uvqk = jnp.concatenate([dense[i * D : i * D + D] for i in range(1, 5)], 1).astype(F32)
    uvqk_step, uvqk_m_new, uvqk_v_new = adam_update(
        uvqk_weight, sum_uvqk, uvqk_m, uvqk_v, WEIGHT_DECAY
    )
    out_step, out_m_new, out_v_new = adam_update(out_weight, sum_out, out_m, out_v, WEIGHT_DECAY)
    bias_step, bias_m_new, bias_v_new = adam_update(time_bias, sum_bias, bias_m, bias_v, 0.0)
    gain_step, gain_m_new, gain_v_new = adam_update(gains, sum_gains, gain_m, gain_v, 0.0)
    return (
        new_table,
        new_acc,
        uvqk_step,
        uvqk_m_new,
        uvqk_v_new,
        out_step,
        out_m_new,
        out_v_new,
        bias_step,
        bias_m_new,
        bias_v_new,
        gain_step,
        gain_m_new,
        gain_v_new,
        summary,
        attention_rms,
    )


def solution(mesh):
    sizes = (mesh.shape["dp"], mesh.shape["mp"])
    bits = [size.bit_length() - 1 for size in sizes]
    axes = tuple(f"d{i}" for i in range(bits[0])) + tuple(f"m{i}" for i in range(bits[1]))
    fine = Mesh(mesh.devices.reshape((2,) * len(axes)), axes)
    split = P(axes)
    whole = P()

    def body(*args):
        return per_device(axes, *args)

    return jax.shard_map(
        body,
        mesh=fine,
        in_specs=(split, split) + (whole,) * 12 + (split,) * 4,
        out_specs=(split, split) + (whole,) * 14,
        check_vma=False,
    )
```

```python
import functools
import math

import jax
import jax.numpy as jnp
from jax import lax
from jax.experimental import pallas as pl
from jax.experimental.pallas import tpu as pltpu
from jax.sharding import Mesh
from jax.sharding import PartitionSpec as P


D = 512
H = 8
NB = 32

EPSILON = 1e-06
ROW_RATE = 0.2
LEARN_RATE = 0.01
BETA_ONE = 0.9
BETA_TWO = 0.95
ADAM_EPSILON = 1e-08
WEIGHT_DECAY = 0.1

SWAP = [(0, 1), (1, 0)]
BLK = 256
F32 = jnp.float32
BF16 = jnp.bfloat16
HIGH = lax.Precision.HIGHEST
PARAMS = pltpu.CompilerParams(vmem_limit_bytes=16 * 1024 * 1024)
BIG_PARAMS = pltpu.CompilerParams(vmem_limit_bytes=63 * 1024 * 1024)
NT = (((1,), (1,)), ((), ()))
TN = (((0,), (0,)), ((), ()))


def dot(left, right):
    return jnp.dot(left, right, preferred_element_type=F32)


def dot_nt(left, right):
    return lax.dot_general(left, right, NT, preferred_element_type=F32)


def dot_tn(left, right):
    return lax.dot_general(left, right, TN, preferred_element_type=F32)


def iota(shape, dim):
    return lax.broadcasted_iota(jnp.int32, shape, dim)


def one_hot(mask):
    return jnp.where(mask, 1.0, 0.0).astype(BF16)


def at(block):
    return pl.ds(pl.multiple_of(block * BLK, BLK), BLK)


def root_mean(mean_square):
    return jnp.sqrt(mean_square + EPSILON)


def mean_last(values):
    return jnp.mean(values, -1, keepdims=True)


def sds(*shape, dtype=BF16):
    return jax.ShapeDtypeStruct(shape, dtype)


def adam_update(weight, gradient, first, second, decay):
    first_new = BETA_ONE * first + (1.0 - BETA_ONE) * gradient
    second_new = BETA_TWO * second + (1.0 - BETA_TWO) * gradient * gradient
    update = -LEARN_RATE * (first_new / (jnp.sqrt(second_new) + ADAM_EPSILON) + decay * weight)
    return (update, first_new, second_new)


def upright(row, size, offset=0):
    spot = iota((size, row.shape[1]), 1) == iota((size, row.shape[1]), 0) + offset
    return jnp.sum(jnp.where(spot, row, 0.0), 1, keepdims=True)


def slots_kernel(devices, capacity, half_ref, owner_ref, rows_ref, slotc_ref, slotr_ref, ids_ref):
    requests = owner_ref.shape[1]
    peers = devices // 2
    wide = rows_ref.shape[1]
    relative = owner_ref[...] - half_ref[0] * peers
    relative = jnp.where(relative < 0, relative + devices, relative)
    upper = one_hot(iota((BLK, BLK), 0) < iota((BLK, BLK), 1))
    run = jnp.zeros((devices, 1), F32)
    acc_hi = jnp.zeros((peers, 2 * capacity), F32)
    acc_lo = jnp.zeros((peers, 2 * capacity), F32)
    for block in range(requests // BLK):
        part = slice(block * BLK, (block + 1) * BLK)
        owner = relative[:, part]
        hits = jnp.where(owner == iota((devices, BLK), 0), 1.0, 0.0)
        before = dot(hits.astype(BF16), upper) + run
        rank = jnp.sum(before * hits, 0, keepdims=True)
        run = run + jnp.sum(hits, 1, keepdims=True)
        slot = owner.astype(F32) * capacity + rank
        slotr_ref[:, part] = slot.astype(jnp.int32)
        slotc_ref[part, :] = upright(slot, BLK).astype(jnp.int32)
        far = owner >= peers
        place_at = upright(rank + jnp.where(far, 1.0 * capacity, 0.0), BLK)
        where = one_hot(iota((BLK, 2 * capacity), 1) == place_at.astype(jnp.int32))
        mine = jnp.where(far, owner - peers, owner) == iota((peers, BLK), 0)
        rows = [rows_ref[i : i + 1, :] for i in range(block * BLK // wide, (block + 1) * BLK // wide)]
        rows = jnp.concatenate(rows, 1)
        hi = rows // 32
        lo = rows - hi * 32
        acc_hi = acc_hi + dot(jnp.where(mine, hi.astype(F32), 0.0).astype(BF16), where)
        acc_lo = acc_lo + dot(jnp.where(mine, lo.astype(F32), 0.0).astype(BF16), where)
    ids_ref[:, 0, :] = (acc_hi * 32.0 + acc_lo).astype(jnp.int32)


def request_slots(half, owners, item_rows, devices, capacity):
    requests = item_rows.shape[0]
    vmem = pl.BlockSpec(memory_space=pltpu.VMEM)
    return pl.pallas_call(
        functools.partial(slots_kernel, devices, capacity),
        out_shape=(
            sds(requests, 1, dtype=jnp.int32),
            sds(1, requests, dtype=jnp.int32),
            sds(devices // 2, 1, 2 * capacity, dtype=jnp.int32),
        ),
        in_specs=[pl.BlockSpec(memory_space=pltpu.SMEM)] + [vmem] * 2,
        out_specs=[vmem] * 3,
        compiler_params=BIG_PARAMS,
        name="request_slots",
    )(half, owners.reshape(1, requests), item_rows.reshape(requests // 128, 128))


def serve_kernel(offset, ids_ref, *refs):
    *table_refs, out_ref, hits = refs
    rows = table_refs[0].shape[0]
    table = table_refs[0][...]
    for other in table_refs[1:]:
        table = table + other[...]
    peers = ids_ref.shape[0]
    capacity = out_ref.shape[0] // peers
    for peer in range(peers):
        ids = upright(ids_ref[peer].astype(F32), capacity, offset).astype(jnp.int32)
        hits[peer * capacity : (peer + 1) * capacity, :] = one_hot(ids == iota((capacity, rows), 1))
    size = out_ref.shape[0] // 3
    for block in range(3):
        part = slice(block * size, (block + 1) * size)
        out_ref[part, :] = dot(hits[part, :], table).astype(BF16)


def serve(ids, tables, offset):
    slots = ids.shape[0] * (ids.shape[2] // 2)
    rows, width = tables[0].shape
    return pl.pallas_call(
        functools.partial(serve_kernel, offset),
        out_shape=sds(slots, width),
        scratch_shapes=[pltpu.VMEM((slots, rows), BF16)],
        compiler_params=PARAMS,
        name="serve",
    )(ids, *tables)


def place_kernel(slotc_ref, got_ref, out_ref):
    slots = got_ref.shape[0]
    for block in range(out_ref.shape[0] // BLK):
        part = slice(block * BLK, (block + 1) * BLK)
        hits = one_hot(slotc_ref[part, :] == iota((BLK, slots), 1))
        out_ref[part, :] = dot(hits, got_ref[...]).astype(BF16)


def place(slotc, got):
    return pl.pallas_call(
        place_kernel,
        out_shape=sds(slotc.shape[0], got.shape[1]),
        compiler_params=PARAMS,
        name="place",
    )(slotc, got)


def step_kernel(
    total_tokens,
    len_ref,
    core_ref,
    own_ref,
    far_ref,
    slotc_ref,
    slotr_ref,
    w_ref,
    wo_ref,
    gains_ref,
    tb_ref,
    bucketr_ref,
    bucketc_ref,
    out_ref,
    rows_ref,
    keep_ref,
    give_ref,
    dbias_ref,
    stats_ref,
    dgain_ref,
    n1_ref,
    dp_ref,
    xs,
    neg,
    gate,
    deriv_ref,
    att,
    v_ref,
    q_ref,
    k_ref,
    baug,
    do_ref,
    abuf,
    sbuf,
    dnacc,
    dwo,
    carry,
    qt,
    dt,
    kt,
    vt,
    dkb,
):
    seq_len = n1_ref.shape[0]
    requests = rows_ref.shape[0]
    negs = requests - seq_len
    slots = far_ref.shape[0]
    blocks = seq_len // BLK
    length = len_ref[0]
    inv_len = 1.0 / (jnp.zeros((1, 1), jnp.int32) + length).astype(F32)

    def fetch(block):
        hits = one_hot(slotc_ref[at(block), :] - slots == iota((BLK, slots), 1))
        return own_ref[at(block), :].astype(F32) + dot(hits, far_ref[...])

    xs[pl.ds(seq_len, 8), :] = jnp.zeros((8, D), F32)
    tb = 0.5 * tb_ref[...]
    tb_hi = tb.astype(BF16)
    tb_lo = (tb - tb_hi.astype(F32)).astype(BF16)
    head = iota((H, D), 0)
    spot = head // 2 * 128 + jnp.where(head % 2 == 0, 64, 0)
    lane_of = iota((H, D), 1)
    terms = dot_tn(tb_hi, one_hot(lane_of == spot)) + dot_tn(tb_lo, one_hot(lane_of == spot + 1))
    terms = terms.astype(BF16)

    def project(block, sum_x):
        rows = at(block)
        x = fetch(block)
        xs[rows, :] = x
        baug[rows, :] = dot(one_hot(bucketc_ref[rows, :] == iota((BLK, NB), 1)), terms).astype(BF16)
        mean_sq = mean_last(x * x)
        pos = block * BLK + iota((BLK, 1), 0)
        live = pos < length
        n1 = (x * lax.rsqrt(mean_sq + EPSILON) * gains_ref[0:1, :]).astype(BF16)
        n1_ref[rows, :] = n1
        for part in range(4):
            half_pre = dot(n1, w_ref[:, part * D : (part + 1) * D])
            th = jnp.tanh(half_pre)
            bend = half_pre * th
            act = half_pre + bend
            deriv_ref[rows, part * D : (part + 1) * D] = ((1.0 + th) * (1.0 + half_pre - bend)).astype(BF16)
            if part == 0:
                gate[rows, :] = act
            elif part == 1:
                v_ref[rows, :] = jnp.where(live, act, 0.0).astype(BF16)
            elif part == 2:
                q_ref[rows, :] = (act * (0.5 * (D // H) ** -0.5)).astype(BF16)
            else:
                k_ref[rows, :] = act.astype(BF16)
        return sum_x + jnp.sum(jnp.where(live, root_mean(mean_sq), 0.0), keepdims=True)

    sum_x = lax.fori_loop(0, blocks, project, jnp.zeros((1, 1), F32))

    def fetch_neg(block, _):
        neg[at(block), :] = fetch(blocks + block).astype(BF16)
        return 0

    lax.fori_loop(0, negs // BLK, fetch_neg, 0)

    lower = iota((BLK, BLK), 0) >= iota((BLK, BLK), 1)
    lane = iota((1, 128), 1)
    sides = [one_hot(lane < 64), one_hot(lane >= 64)]
    marks = [one_hot(lane // 2 == 32), one_hot(lane // 2 == 0)]

    def attend(pair, _):
        lanes = pl.ds(pl.multiple_of(pair * 128, 128), 128)
        bias = baug[:, lanes]
        keys = [k_ref[:, lanes] * sides[hh] + bias * sides[1 - hh] for hh in range(2)]
        vals = [v_ref[:, lanes] * sides[hh] for hh in range(2)]
        for qb in range(blocks):
            qs = slice(qb * BLK, (qb + 1) * BLK)
            total = jnp.zeros((BLK, 128), F32)
            for hh in range(2):
                query = q_ref[qs, lanes] * sides[hh] + marks[hh]
                for kb in range(qb + 1):
                    span = slice(kb * BLK, (kb + 1) * BLK)
                    half_s = dot_nt(query, keys[hh][span])
                    th = jnp.tanh(half_s)
                    bend = half_s * th
                    score = half_s + bend
                    deriv = (1.0 + th) * (1.0 + half_s - bend)
                    if kb == qb:
                        score = jnp.where(lower, score, 0.0)
                        deriv = jnp.where(lower, deriv, 0.0)
                    low = score.astype(BF16)
                    tile = qb * (qb + 1) // 2 + kb
                    abuf[2 * pair + hh, tile] = low
                    sbuf[2 * pair + hh, tile] = deriv.astype(BF16)
                    total = total + dot(low, vals[hh][span])
            att[qs, lanes] = total * inv_len
        return 0

    lax.fori_loop(0, H // 2, attend, 0)

    scale = 2.0 / math.sqrt(D)
    dnacc[...] = jnp.zeros_like(dnacc)
    dwo[...] = jnp.zeros_like(dwo)
    carry[...] = jnp.zeros_like(carry)
    first_row = iota((BLK, 1), 0) == 0
    last_row = iota((BLK, 1), 0) == BLK - 1

    def middle(block, sums):
        sum_loss, sum_o, sum_b, dg1, dg2 = sums
        rows = at(block)
        x = xs[rows, :]
        pos = block * BLK + iota((BLK, 1), 0)
        live = pos < length
        valid = pos < length - 1
        o = att[rows, :]
        u = gate[rows, :]
        ms_o = mean_last(o * o)
        r2 = lax.rsqrt(ms_o + EPSILON)
        n2 = o * r2 * gains_ref[1:2, :]
        g = (n2 * u).astype(BF16)
        branch = dot(g, wo_ref[...])
        ms_b = mean_last(branch * branch)
        mixed = x + branch
        r3 = lax.rsqrt(mean_last(mixed * mixed) + EPSILON)
        final = (mixed * r3 * gains_ref[2:3, :]).astype(BF16)
        final_f = final.astype(F32)
        after = xs[pl.ds(pl.multiple_of(block * BLK + BLK, 8), 8), :][0:1, :]
        nxt = jnp.where(last_row, after, pltpu.roll(x, BLK - 1, 0))
        target = jnp.sum(final_f * nxt, -1, keepdims=True) * scale
        logits = dot_nt(final, neg[...]) * scale
        top = jnp.maximum(jnp.max(logits, -1, keepdims=True), target)
        powers = jnp.exp(logits - top)
        near = jnp.exp(target - top)
        total = near + jnp.sum(powers, -1, keepdims=True)
        lse = top + jnp.log(total)
        weight = jnp.where(valid, 1.0 / total_tokens, 0.0)
        share = weight / total
        dt_ = (share * near - weight) * scale
        dz = (share * powers).astype(BF16)
        dfin = dt_ * nxt + scale * dot(dz, neg[...])
        dnacc[...] += dot_tn(dz, final)
        dnext = dt_ * final_f
        shifted = jnp.where(first_row, carry[0:1, :], pltpu.roll(dnext, 1, 0))
        carry[...] = jnp.broadcast_to(dnext[BLK - 1 : BLK, :], carry.shape)
        unit3 = mixed * r3
        dg2 = dg2 + jnp.sum(dfin * unit3, 0, keepdims=True)
        scaled = dfin * gains_ref[2:3, :]
        dy = r3 * (scaled - unit3 * mean_last(scaled * unit3))
        att[rows, :] = dy + shifted
        db = dy.astype(BF16)
        dwo[...] += dot_tn(g, db)
        dg = dot_nt(db, wo_ref[...])
        dp_ref[rows, 0:D] = (0.5 * dg * n2 * deriv_ref[rows, 0:D].astype(F32)).astype(BF16)
        dn2 = dg * u
        unit2 = o * r2
        dg1 = dg1 + jnp.sum(dn2 * unit2, 0, keepdims=True)
        scaled2 = dn2 * gains_ref[1:2, :]
        do = (r2 * (0.5 * inv_len)) * (scaled2 - unit2 * mean_last(scaled2 * unit2))
        do_ref[rows, :] = do.astype(BF16)
        return (
            sum_loss + jnp.sum(jnp.where(valid, lse - target, 0.0), keepdims=True),
            sum_o + jnp.sum(jnp.where(live, root_mean(ms_o), 0.0), keepdims=True),
            sum_b + jnp.sum(jnp.where(live, root_mean(ms_b), 0.0), keepdims=True),
            dg1,
            dg2,
        )

    zero = jnp.zeros((1, 1), F32)
    zrow = jnp.zeros((1, D), F32)
    sum_loss, sum_o, sum_b, dg1, dg2 = lax.fori_loop(0, blocks, middle, (zero, zero, zero, zrow, zrow))
    rows_ref[seq_len:requests, :] = (dnacc[...] * scale).astype(BF16)
    which = iota((8, 128), 0)
    stats = jnp.where(which == 0, sum_loss, 0.0) + jnp.where(which == 1, sum_x, 0.0)
    stats_ref[...] = stats + jnp.where(which == 2, sum_o, 0.0) + jnp.where(which == 3, sum_b, 0.0)

    ones = one_hot(iota((16, seq_len), 0) == 0)
    alive = iota((seq_len, 1), 0) < length

    def attend_back(pair, _):
        lanes = pl.ds(pl.multiple_of(pair * 128, 128), 128)
        keys = [k_ref[:, lanes] * side for side in sides]
        vals = [v_ref[:, lanes] * side for side in sides]
        grads = do_ref[:, lanes]
        qtr = q_ref[:, lanes].astype(F32).T.astype(BF16)
        dtr = grads.astype(F32).T.astype(BF16)
        for hh in range(2):
            qt[hh, 0:64, :] = qtr[hh * 64 : hh * 64 + 64, :]
            qt[hh, 64:80, :] = ones
            dt[hh] = dtr[hh * 64 : hh * 64 + 64, :]
        kt[...] = jnp.zeros_like(kt)
        vt[...] = jnp.zeros_like(vt)
        dql = pl.ds(pl.multiple_of(2 * D + pair * 128, 128), 128)
        for qb in range(blocks):
            qs = slice(qb * BLK, (qb + 1) * BLK)
            dq = jnp.zeros((BLK, 128), F32)
            for hh in range(2):
                for kb in range(qb + 1):
                    span = slice(kb * BLK, (kb + 1) * BLK)
                    tile = qb * (qb + 1) // 2 + kb
                    slope = sbuf[2 * pair + hh, tile].astype(F32)
                    ds = (dot_nt(grads[qs], vals[hh][span]) * slope).astype(BF16)
                    dq = dq + dot(ds, keys[hh][span])
                    kt[hh, :, span] += dot(qt[hh, :, qs], ds)
                    vt[hh, :, span] += dot(dt[hh, :, qs], abuf[2 * pair + hh, tile])
            dq = dq * (0.5 * (D // H) ** -0.5)
            dp_ref[qs, dql] = (dq * deriv_ref[qs, dql].astype(F32)).astype(BF16)
        dkl = pl.ds(pl.multiple_of(3 * D + pair * 128, 128), 128)
        dvl = pl.ds(pl.multiple_of(D + pair * 128, 128), 128)
        dk = jnp.concatenate([kt[0, 0:64, :], kt[1, 0:64, :]], 0).T
        dv = jnp.concatenate([vt[0], vt[1]], 0).T
        dp_ref[:, dkl] = (dk * deriv_ref[:, dkl].astype(F32)).astype(BF16)
        dp_ref[:, dvl] = (jnp.where(alive, dv, 0.0) * deriv_ref[:, dvl].astype(F32)).astype(BF16)
        for hh in range(2):
            dkb[pl.ds(2 * pair + hh, 1), :] = kt[hh, 64:65, :]
        return 0

    lax.fori_loop(0, H // 2, attend_back, 0)
    buckets = jnp.where(bucketr_ref[...] == iota((NB, seq_len), 0), 1.0, 0.0)
    dbias_ref[...] = lax.dot_general(dkb[...], buckets, NT, precision=HIGH, preferred_element_type=F32)

    def tail(block, dg0):
        rows = at(block)
        x = xs[rows, :]
        r1 = lax.rsqrt(mean_last(x * x) + EPSILON)
        unit1 = x * r1
        dn1 = dot_nt(dp_ref[rows, :], w_ref[...])
        dg0 = dg0 + jnp.sum(dn1 * unit1, 0, keepdims=True)
        scaled = dn1 * (2.0 * gains_ref[0:1, :])
        dx = r1 * (scaled - unit1 * mean_last(scaled * unit1)) + att[rows, :]
        rows_ref[rows, :] = dx.astype(BF16)
        return dg0

    dg0 = 2.0 * lax.fori_loop(0, blocks, tail, zrow)
    row = iota((8, D), 0)
    gsum = jnp.where(row == 0, dg0, 0.0) + jnp.where(row == 1, dg1, 0.0)
    dgain_ref[...] = gsum + jnp.where(row == 2, dg2, 0.0)

    def put(block, _):
        slot = slots + block * BLK + iota((BLK, 1), 0)
        out_ref[at(block), :] = dot(one_hot(slotr_ref[...] == slot), rows_ref[...]).astype(BF16)
        return 0

    lax.fori_loop(0, slots // BLK, put, 0)

    half = keep_ref.shape[0] // BLK

    def write(block, values):
        rows = slice(block % half * BLK, (block % half + 1) * BLK)

        @pl.when(core_ref[0] == block // half)
        def _():
            keep_ref[rows, :] = values

        @pl.when(core_ref[0] != block // half)
        def _():
            give_ref[rows, :] = values

    for side in range(D // BLK):
        rows = slice(side * BLK, (side + 1) * BLK)
        write(side, dwo[rows, :].astype(BF16))
        turned = n1_ref[:, rows].astype(F32).T.astype(BF16)
        for part in range(4):
            grad = dot(turned, dp_ref[:, part * D : (part + 1) * D])
            write((part + 1) * (D // BLK) + side, grad.astype(BF16))


def step(length, core, own, far, slotc, slotr, w, wo, gains, time_bias, buckets, total_tokens):
    seq_len = buckets.shape[1]
    requests = slotc.shape[0]
    negs = requests - seq_len
    slots = far.shape[0]
    vmem = pl.BlockSpec(memory_space=pltpu.VMEM)
    blocks = seq_len // BLK
    tiles = blocks * (blocks + 1) // 2
    outs = (
        sds(slots, D),
        sds(requests, D),
        sds(5 * D // 2, D),
        sds(5 * D // 2, D),
        sds(H, NB, dtype=F32),
        sds(8, 128, dtype=F32),
        sds(8, D, dtype=F32),
    )
    return pl.pallas_call(
        functools.partial(step_kernel, total_tokens),
        out_shape=outs,
        in_specs=[pl.BlockSpec(memory_space=pltpu.SMEM)] * 2 + [vmem] * 10,
        out_specs=[vmem] * len(outs),
        scratch_shapes=[
            pltpu.VMEM((seq_len, D), BF16),
            pltpu.VMEM((seq_len, 4 * D), BF16),
            pltpu.VMEM((seq_len + 8, D), F32),
            pltpu.VMEM((negs, D), BF16),
            pltpu.VMEM((seq_len, D), F32),
            pltpu.VMEM((seq_len, 4 * D), BF16),
            pltpu.VMEM((seq_len, D), F32),
            pltpu.VMEM((seq_len, D), BF16),
            pltpu.VMEM((seq_len, D), BF16),
            pltpu.VMEM((seq_len, D), BF16),
            pltpu.VMEM((seq_len, D), BF16),
            pltpu.VMEM((seq_len, D), BF16),
            pltpu.VMEM((H, tiles, BLK, BLK), BF16),
            pltpu.VMEM((H, tiles, BLK, BLK), BF16),
            pltpu.VMEM((negs, D), F32),
            pltpu.VMEM((D, D), F32),
            pltpu.VMEM((8, D), F32),
            pltpu.VMEM((2, 80, seq_len), BF16),
            pltpu.VMEM((2, 64, seq_len), BF16),
            pltpu.VMEM((2, 80, seq_len), F32),
            pltpu.VMEM((2, 64, seq_len), F32),
            pltpu.VMEM((H, seq_len), F32),
        ],
        compiler_params=BIG_PARAMS,
        cost_estimate=pl.CostEstimate(flops=50_000_000_000, bytes_accessed=15_000_000, transcendentals=0),
        name="step",
    )(length, core, own, far, slotc, slotr, w, wo, gains, time_bias, buckets, buckets.reshape(seq_len, 1))


def spread_kernel(slotr_ref, rows_ref, out_ref):
    def put(block, _):
        slot = block * BLK + iota((BLK, 1), 0)
        out_ref[at(block), :] = dot(one_hot(slotr_ref[...] == slot), rows_ref[...]).astype(BF16)
        return 0

    lax.fori_loop(0, out_ref.shape[0] // BLK, put, 0)


def spread(slotr, rows, slots):
    return pl.pallas_call(
        spread_kernel,
        out_shape=sds(slots, D),
        compiler_params=PARAMS,
        name="spread",
    )(slotr, rows)


def gather_kernel(ids_ref, got_ref, out_ref):
    rows, slots = (out_ref.shape[0], got_ref.shape[0])
    hits = one_hot(ids_ref[...] == iota((rows, slots), 0))
    out_ref[...] = dot(hits, got_ref[...]).astype(BF16)


def row_sums(ids, got, rows):
    return pl.pallas_call(
        gather_kernel,
        out_shape=sds(rows, got.shape[1]),
        compiler_params=PARAMS,
        name="row_sums",
    )(ids, got)


def update_kernel(ids_ref, got_ref, far_ref, table_ref, acc_ref, table_out, acc_out):
    rows, slots = (table_ref.shape[0], got_ref.shape[0])
    hits = one_hot(ids_ref[...] == iota((rows, slots), 0))
    sums = dot(hits, got_ref[...]) + far_ref[...].astype(F32)
    acc = acc_ref[...] + mean_last(sums * sums)
    acc_out[...] = acc
    table_out[...] = table_ref[...] - ROW_RATE * sums * lax.rsqrt(acc)


def update_rows(ids, got, far, table, row_acc):
    rows = table.shape[0]
    new_table, new_acc = pl.pallas_call(
        update_kernel,
        out_shape=(sds(*table.shape, dtype=F32), sds(rows, 1, dtype=F32)),
        compiler_params=PARAMS,
        name="update_rows",
    )(ids, got, far, table, row_acc.reshape(rows, 1))
    return new_table, new_acc.reshape(rows)


def pick(array, index, dim):
    return lax.dynamic_index_in_dim(array, index, dim, keepdims=False)


def swap(values, axis):
    return lax.ppermute(values, axis, SWAP)


def add(left, right):
    return (left.astype(F32) + right.astype(F32)).astype(BF16)


def turn(values, axes, stage):
    pairs = []
    for place in range(8):
        core = place & 1
        flip = 4 if core == stage else 2
        pairs.append((place, place ^ flip))
    return lax.ppermute(values, axes, pairs)


def sum_chips(keep, got, order, pair):
    rows, width = keep.shape
    one = lax.axis_index(pair) == 0
    here, there = (lax.axis_index(order[0]), lax.axis_index(order[1]))
    outer = jnp.where(one, here, there)
    inner = jnp.where(one, there, here)
    plane = order[:2] + (pair,)
    terms = [values.reshape(2, 2, rows // 4, width) for values in (keep, got)]
    got = turn(add(*[pick(v, 1 - outer, 0) for v in terms]), plane, 0)
    terms = [add(*[pick(v, outer, 0) for v in terms]), got]
    got = turn(add(*[pick(v, 1 - inner, 0) for v in terms]), plane, 1)
    part = add(add(*[pick(v, inner, 0) for v in terms]), got)
    for axis in order[2:]:
        part = part.reshape(2, part.shape[0] // 2, width)
        here = lax.axis_index(axis)
        got = swap(pick(part, 1 - here, 0), axis)
        part = add(pick(part, here, 0), got)
    return part


def join(values, got, first):
    return jnp.stack([jnp.where(first, values, got), jnp.where(first, got, values)])


def share_chips(part, extra, order, pair):
    rows, width = part.shape
    packed = jnp.concatenate([part, extra], 0)
    for axis in reversed(order[2:]):
        packed = join(packed, swap(packed, axis), lax.axis_index(axis) == 0)
    one = lax.axis_index(pair) == 0
    here, there = (lax.axis_index(order[0]), lax.axis_index(order[1]))
    plane = order[:2] + (pair,)
    packed = packed.reshape(-1, rows + extra.shape[0], width)
    inner, outer = (jnp.where(one, there, here), jnp.where(one, here, there))
    packed = join(packed, turn(packed, plane, 1), inner == 0)
    packed = join(packed, turn(packed, plane, 0), outer == 0)
    whole = packed.reshape(-1, rows + extra.shape[0], width)
    return whole[:, :rows].reshape(-1, width), whole[:, rows:]


def adam_kernel(core_ref, mine_ref, other_ref, *refs):
    sources, targets, inside_, outside, sem_in, sem_out = (refs[:6], refs[6:12], refs[12:18], refs[18:24], *refs[24:])
    chunks = sem_in.shape[0]
    size = D // chunks
    half = mine_ref.shape[0] // size
    parts = 1 + sources[0].shape[1] // D

    def copy(chunk, k, incoming):
        rows = pl.ds(pl.multiple_of(chunk * size, size), size)
        if incoming:
            return pltpu.make_async_copy(sources[k].at[rows], inside_[k].at[rows], sem_in.at[chunk, k])
        return pltpu.make_async_copy(outside[k].at[rows], targets[k].at[rows], sem_out.at[chunk, k])

    def begin(chunk, _):
        for k in range(6):
            copy(chunk, k, True).start()
        return 0

    lax.fori_loop(0, chunks, begin, 0)

    def compute(chunk, _):
        for k in range(6):
            copy(chunk, k, True).wait()
        rows = pl.ds(pl.multiple_of(chunk * size, size), size)
        for part in range(parts):
            spot = part * chunks + chunk
            from_ = pl.ds(pl.multiple_of(lax.rem(spot, half) * size, size), size)
            own = spot // half == core_ref[0]
            grad = jnp.where(own, mine_ref[from_, :].astype(F32), other_ref[from_, :].astype(F32))
            first = 0 if part else 3
            columns = slice((part - 1) * D, part * D) if part else slice(None)
            w, m, v = (inside_[first + k][rows, columns] for k in range(3))
            for k, value in enumerate(adam_update(w, grad, m, v, WEIGHT_DECAY)):
                outside[first + k][rows, columns] = value
        for k in range(6):
            copy(chunk, k, False).start()
        return 0

    lax.fori_loop(0, chunks, compute, 0)

    def finish(chunk, _):
        for k in range(6):
            copy(chunk, k, False).wait()
        return 0

    lax.fori_loop(0, chunks, finish, 0)


def adam(core, mine, other, uvqk, out):
    chunks = 8
    vmem = pl.BlockSpec(memory_space=pltpu.VMEM)
    hbm = pl.BlockSpec(memory_space=pl.ANY)
    shapes = [uvqk[0].shape] * 3 + [out[0].shape] * 3
    buffers = [pltpu.VMEM(shape, F32) for shape in shapes]
    return pl.pallas_call(
        adam_kernel,
        out_shape=[sds(*shape, dtype=F32) for shape in shapes],
        in_specs=[pl.BlockSpec(memory_space=pltpu.SMEM), vmem, vmem] + [hbm] * 6,
        out_specs=[hbm] * 6,
        scratch_shapes=buffers
        + buffers
        + [pltpu.SemaphoreType.DMA((chunks, 6)), pltpu.SemaphoreType.DMA((chunks, 6))],
        compiler_params=BIG_PARAMS,
        name="adam",
    )(core, mine, other, *uvqk, *out)


def per_device(
    axes,
    table,
    row_acc,
    uvqk_weight,
    out_weight,
    time_bias,
    gains,
    uvqk_m,
    uvqk_v,
    out_m,
    out_v,
    bias_m,
    bias_v,
    gain_m,
    gain_v,
    lengths,
    time_buckets,
    item_rows,
    row_owner,
):
    every = axes
    near = axes[1:]
    devices = lax.axis_size(every)
    peers = devices // 2
    requests = item_rows.shape[0]
    capacity = max(2, 2 * requests // devices)
    rows = table.shape[0]
    slots = peers * capacity
    total_tokens = float(time_buckets.size * devices)
    half = lax.axis_index(axes[0]).reshape(1)
    core = lax.axis_index(axes[-1]).reshape(1)

    def exchange(values):
        return lax.all_to_all(values.reshape(peers, capacity, D), near, 0, 0, tiled=True).reshape(slots, D)

    table_low = table.astype(BF16)
    slotc, slotr, ids = request_slots(half, row_owner, item_rows, devices, capacity)
    ids = lax.all_to_all(ids, near, 0, 0, tiled=True)
    ids_own = ids[:, 0, :capacity]
    ids_far = ids[:, 0, capacity:]
    outer = lax.ppermute(table_low, axes[:2], [(0, 2), (3, 1)])
    inner = lax.ppermute(table_low, axes[:2], [(1, 3), (2, 0)])
    serve_own = serve(ids, [table_low], 0)
    got_own = exchange(serve_own)
    serve_far = serve(ids, [outer, inner], capacity)
    got_far = exchange(serve_far)
    own = place(slotc, got_own)

    w_low = (0.5 * uvqk_weight).astype(BF16)
    wo_low = out_weight.astype(BF16)
    send_far, row_grads, keep, give, dbias, stats, dgain = step(
        lengths, core, own, got_far, slotc, slotr, w_low, wo_low, gains, time_bias, time_buckets, total_tokens
    )
    back_far = exchange(send_far)
    send_own = spread(slotr, row_grads, slots)
    got = swap(give, axes[-1])
    order = axes[-3:-1] + axes[-4::-1]
    unit = 8 << len(order)
    pad = -keep.shape[0] % unit
    part = sum_chips(*[jnp.pad(v, ((0, pad), (0, 0))) for v in (keep, got)], order, axes[-1])
    sums_far = row_sums(ids_far.reshape(1, slots), back_far, rows)
    sums_far = lax.ppermute(sums_far, axes[0], SWAP)
    back_own = exchange(send_own)
    new_table, new_acc = update_rows(ids_own.reshape(1, slots), back_own, sums_far, table, row_acc)

    small = jnp.concatenate(
        [
            dbias.reshape(-1),
            dgain[:3].reshape(-1),
            stats[:4, 0],
            jnp.zeros((2048 - H * NB - 3 * D - 4,), F32),
        ]
    ).reshape(4, D)
    small = small + lax.ppermute(small, axes[-1], SWAP)
    small_hi = lax.reduce_precision(small, 8, 7)
    small_lo = (small - small_hi).astype(BF16)
    small_hi = small_hi.astype(BF16)
    mine, small = share_chips(part, jnp.concatenate([small_hi, small_lo], 0), order, axes[-1])
    mine = mine[: keep.shape[0]]
    other = swap(mine, axes[-1])
    small = jnp.sum(small.astype(F32), 0)
    small = (small[:4] + small[4:]).reshape(-1)
    sum_bias = small[: H * NB].reshape(H, NB)
    sum_gains = small[H * NB : H * NB + 3 * D].reshape(3, D)
    sums = small[H * NB + 3 * D : H * NB + 3 * D + 4] / total_tokens
    summary = jnp.stack([sums[0], sums[1], sums[3]])
    attention_rms = sums[2:3]

    uvqk_step, uvqk_m_new, uvqk_v_new, out_step, out_m_new, out_v_new = adam(
        core, mine, other, (uvqk_weight, uvqk_m, uvqk_v), (out_weight, out_m, out_v)
    )
    bias_step, bias_m_new, bias_v_new = adam_update(time_bias, sum_bias, bias_m, bias_v, 0.0)
    gain_step, gain_m_new, gain_v_new = adam_update(gains, sum_gains, gain_m, gain_v, 0.0)
    return (
        new_table,
        new_acc,
        uvqk_step,
        uvqk_m_new,
        uvqk_v_new,
        out_step,
        out_m_new,
        out_v_new,
        bias_step,
        bias_m_new,
        bias_v_new,
        gain_step,
        gain_m_new,
        gain_v_new,
        summary,
        attention_rms,
    )


def solution(mesh):
    sizes = (mesh.shape["dp"], mesh.shape["mp"])
    bits = [size.bit_length() - 1 for size in sizes]
    axes = tuple(f"d{i}" for i in range(bits[0])) + tuple(f"m{i}" for i in range(bits[1]))
    fine = Mesh(mesh.devices.reshape((2,) * len(axes)), axes)
    split = P(axes)
    whole = P()

    def body(*args):
        return per_device(axes, *args)

    return jax.shard_map(
        body,
        mesh=fine,
        in_specs=(split, split) + (whole,) * 12 + (split,) * 4,
        out_specs=(split, split) + (whole,) * 14,
        check_vma=False,
    )
```

```python
import functools
import math

import jax
import jax.numpy as jnp
from jax import lax
from jax.experimental import pallas as pl
from jax.experimental.pallas import tpu as pltpu
from jax.sharding import Mesh
from jax.sharding import PartitionSpec as P


D = 512
H = 8
NB = 32

EPSILON = 1e-06
ROW_RATE = 0.2
LEARN_RATE = 0.01
BETA_ONE = 0.9
BETA_TWO = 0.95
ADAM_EPSILON = 1e-08
WEIGHT_DECAY = 0.1

SWAP = [(0, 1), (1, 0)]
BLK = 256
F32 = jnp.float32
BF16 = jnp.bfloat16
HIGH = lax.Precision.HIGHEST
PARAMS = pltpu.CompilerParams(vmem_limit_bytes=16 * 1024 * 1024)
BIG_PARAMS = pltpu.CompilerParams(vmem_limit_bytes=63 * 1024 * 1024)
NT = (((1,), (1,)), ((), ()))
TN = (((0,), (0,)), ((), ()))


def dot(left, right):
    return jnp.dot(left, right, preferred_element_type=F32)


def dot_nt(left, right):
    return lax.dot_general(left, right, NT, preferred_element_type=F32)


def dot_tn(left, right):
    return lax.dot_general(left, right, TN, preferred_element_type=F32)


def iota(shape, dim):
    return lax.broadcasted_iota(jnp.int32, shape, dim)


def one_hot(mask):
    return jnp.where(mask, 1.0, 0.0).astype(BF16)


def at(block):
    return pl.ds(pl.multiple_of(block * BLK, BLK), BLK)


def root_mean(mean_square):
    return jnp.sqrt(mean_square + EPSILON)


def mean_last(values):
    return jnp.mean(values, -1, keepdims=True)


def sds(*shape, dtype=BF16):
    return jax.ShapeDtypeStruct(shape, dtype)


def adam_update(weight, gradient, first, second, decay):
    first_new = BETA_ONE * first + (1.0 - BETA_ONE) * gradient
    second_new = BETA_TWO * second + (1.0 - BETA_TWO) * gradient * gradient
    update = -LEARN_RATE * (first_new / (jnp.sqrt(second_new) + ADAM_EPSILON) + decay * weight)
    return (update, first_new, second_new)


def upright(row, size, offset=0):
    spot = iota((size, row.shape[1]), 1) == iota((size, row.shape[1]), 0) + offset
    return jnp.sum(jnp.where(spot, row, 0.0), 1, keepdims=True)


def slots_kernel(devices, capacity, half_ref, owner_ref, rows_ref, slotc_ref, slotr_ref, ids_ref):
    requests = owner_ref.shape[1]
    peers = devices // 2
    wide = rows_ref.shape[1]
    relative = owner_ref[...] - half_ref[0] * peers
    relative = jnp.where(relative < 0, relative + devices, relative)
    upper = one_hot(iota((BLK, BLK), 0) < iota((BLK, BLK), 1))
    run = jnp.zeros((devices, 1), F32)
    acc_hi = jnp.zeros((peers, 2 * capacity), F32)
    acc_lo = jnp.zeros((peers, 2 * capacity), F32)
    for block in range(requests // BLK):
        part = slice(block * BLK, (block + 1) * BLK)
        owner = relative[:, part]
        hits = jnp.where(owner == iota((devices, BLK), 0), 1.0, 0.0)
        before = dot(hits.astype(BF16), upper) + run
        rank = jnp.sum(before * hits, 0, keepdims=True)
        run = run + jnp.sum(hits, 1, keepdims=True)
        slot = owner.astype(F32) * capacity + rank
        slotr_ref[:, part] = slot.astype(jnp.int32)
        slotc_ref[part, :] = upright(slot, BLK).astype(jnp.int32)
        far = owner >= peers
        place_at = upright(rank + jnp.where(far, 1.0 * capacity, 0.0), BLK)
        where = one_hot(iota((BLK, 2 * capacity), 1) == place_at.astype(jnp.int32))
        mine = jnp.where(far, owner - peers, owner) == iota((peers, BLK), 0)
        rows = [rows_ref[i : i + 1, :] for i in range(block * BLK // wide, (block + 1) * BLK // wide)]
        rows = jnp.concatenate(rows, 1)
        hi = rows // 32
        lo = rows - hi * 32
        acc_hi = acc_hi + dot(jnp.where(mine, hi.astype(F32), 0.0).astype(BF16), where)
        acc_lo = acc_lo + dot(jnp.where(mine, lo.astype(F32), 0.0).astype(BF16), where)
    ids_ref[:, 0, :] = (acc_hi * 32.0 + acc_lo).astype(jnp.int32)


def request_slots(half, owners, item_rows, devices, capacity):
    requests = item_rows.shape[0]
    vmem = pl.BlockSpec(memory_space=pltpu.VMEM)
    return pl.pallas_call(
        functools.partial(slots_kernel, devices, capacity),
        out_shape=(
            sds(requests, 1, dtype=jnp.int32),
            sds(1, requests, dtype=jnp.int32),
            sds(devices // 2, 1, 2 * capacity, dtype=jnp.int32),
        ),
        in_specs=[pl.BlockSpec(memory_space=pltpu.SMEM)] + [vmem] * 2,
        out_specs=[vmem] * 3,
        compiler_params=BIG_PARAMS,
        name="request_slots",
    )(half, owners.reshape(1, requests), item_rows.reshape(requests // 128, 128))


def serve_kernel(offset, ids_ref, *refs):
    *table_refs, out_ref, hits = refs
    rows = table_refs[0].shape[0]
    table = table_refs[0][...]
    for other in table_refs[1:]:
        table = table + other[...]
    peers = ids_ref.shape[0]
    capacity = out_ref.shape[0] // peers
    for peer in range(peers):
        ids = upright(ids_ref[peer].astype(F32), capacity, offset).astype(jnp.int32)
        hits[peer * capacity : (peer + 1) * capacity, :] = one_hot(ids == iota((capacity, rows), 1))
    size = out_ref.shape[0] // 3
    for block in range(3):
        part = slice(block * size, (block + 1) * size)
        out_ref[part, :] = dot(hits[part, :], table).astype(BF16)


def serve(ids, tables, offset):
    slots = ids.shape[0] * (ids.shape[2] // 2)
    rows, width = tables[0].shape
    return pl.pallas_call(
        functools.partial(serve_kernel, offset),
        out_shape=sds(slots, width),
        scratch_shapes=[pltpu.VMEM((slots, rows), BF16)],
        compiler_params=PARAMS,
        name="serve",
    )(ids, *tables)


def place_kernel(slotc_ref, got_ref, out_ref):
    slots = got_ref.shape[0]
    for block in range(out_ref.shape[0] // BLK):
        part = slice(block * BLK, (block + 1) * BLK)
        hits = one_hot(slotc_ref[part, :] == iota((BLK, slots), 1))
        out_ref[part, :] = dot(hits, got_ref[...]).astype(BF16)


def place(slotc, got):
    return pl.pallas_call(
        place_kernel,
        out_shape=sds(slotc.shape[0], got.shape[1]),
        compiler_params=PARAMS,
        name="place",
    )(slotc, got)


def step_kernel(
    total_tokens,
    len_ref,
    core_ref,
    own_ref,
    far_ref,
    slotc_ref,
    w_hbm,
    wo_hbm,
    gains_ref,
    tb_ref,
    bucketr_ref,
    bucketc_ref,
    rows_out,
    keep_ref,
    give_ref,
    dbias_ref,
    stats_ref,
    dgain_ref,
    n1_ref,
    dp_ref,
    xs,
    neg,
    gate,
    deriv_ref,
    att,
    v_ref,
    q_ref,
    k_ref,
    baug,
    do_ref,
    abuf,
    sbuf,
    dnacc,
    dwo,
    carry,
    qt,
    dt,
    kt,
    vt,
    dkb,
    w_ref,
    wo_ref,
    rows_ref,
    sems,
):
    seq_len = n1_ref.shape[0]
    requests = rows_ref.shape[0]
    negs = requests - seq_len
    slots = far_ref.shape[0]
    blocks = seq_len // BLK
    length = len_ref[0]
    inv_len = 1.0 / (jnp.zeros((1, 1), jnp.int32) + length).astype(F32)
    copy_w = pltpu.make_async_copy(w_hbm, w_ref, sems.at[0])
    copy_wo = pltpu.make_async_copy(wo_hbm, wo_ref, sems.at[1])
    copy_rows = pltpu.make_async_copy(rows_ref, rows_out, sems.at[2])
    copy_w.start()
    copy_wo.start()

    def fetch(block):
        hits = one_hot(slotc_ref[at(block), :] - slots == iota((BLK, slots), 1))
        return own_ref[at(block), :].astype(F32) + dot(hits, far_ref[...])

    xs[pl.ds(seq_len, 8), :] = jnp.zeros((8, D), F32)
    tb = 0.5 * tb_ref[...]
    tb_hi = tb.astype(BF16)
    tb_lo = (tb - tb_hi.astype(F32)).astype(BF16)
    head = iota((H, D), 0)
    spot = head // 2 * 128 + jnp.where(head % 2 == 0, 64, 0)
    lane_of = iota((H, D), 1)
    terms = dot_tn(tb_hi, one_hot(lane_of == spot)) + dot_tn(tb_lo, one_hot(lane_of == spot + 1))
    terms = terms.astype(BF16)

    def fetch_neg(block, _):
        neg[at(block), :] = fetch(blocks + block).astype(BF16)
        return 0

    lax.fori_loop(0, negs // BLK, fetch_neg, 0)

    def project(block, sum_x):
        rows = at(block)
        x = fetch(block)
        xs[rows, :] = x
        baug[rows, :] = dot(one_hot(bucketc_ref[rows, :] == iota((BLK, NB), 1)), terms).astype(BF16)
        mean_sq = mean_last(x * x)
        pos = block * BLK + iota((BLK, 1), 0)
        live = pos < length
        n1 = (x * lax.rsqrt(mean_sq + EPSILON) * gains_ref[0:1, :]).astype(BF16)
        n1_ref[rows, :] = n1
        for part in range(4):
            half_pre = dot(n1, w_ref[:, part * D : (part + 1) * D])
            th = jnp.tanh(half_pre)
            bend = half_pre * th
            act = half_pre + bend
            deriv_ref[rows, part * D : (part + 1) * D] = ((1.0 + th) * (1.0 + half_pre - bend)).astype(BF16)
            if part == 0:
                gate[rows, :] = act
            elif part == 1:
                v_ref[rows, :] = jnp.where(live, act, 0.0).astype(BF16)
            elif part == 2:
                q_ref[rows, :] = (act * (0.5 * (D // H) ** -0.5)).astype(BF16)
            else:
                k_ref[rows, :] = act.astype(BF16)
        return sum_x + jnp.sum(jnp.where(live, root_mean(mean_sq), 0.0), keepdims=True)

    copy_w.wait()
    copy_wo.wait()
    sum_x = lax.fori_loop(0, blocks, project, jnp.zeros((1, 1), F32))

    def tile_rows(kb, qb):
        start = (kb * blocks - kb * (kb - 1) // 2 + qb - kb) * BLK
        return slice(start, start + BLK)

    lower = iota((BLK, BLK), 0) >= iota((BLK, BLK), 1)
    lane = iota((1, 128), 1)
    sides = [one_hot(lane < 64), one_hot(lane >= 64)]
    marks = [one_hot(lane // 2 == 32), one_hot(lane // 2 == 0)]

    def attend(pair, _):
        lanes = pl.ds(pl.multiple_of(pair * 128, 128), 128)
        bias = baug[:, lanes]
        keys = [k_ref[:, lanes] * sides[hh] + bias * sides[1 - hh] for hh in range(2)]
        vals = [v_ref[:, lanes] * sides[hh] for hh in range(2)]
        for qb in range(blocks):
            qs = slice(qb * BLK, (qb + 1) * BLK)
            total = jnp.zeros((BLK, 128), F32)
            for hh in range(2):
                query = q_ref[qs, lanes] * sides[hh] + marks[hh]
                for kb in range(qb + 1):
                    span = slice(kb * BLK, (kb + 1) * BLK)
                    half_s = dot_nt(query, keys[hh][span])
                    th = jnp.tanh(half_s)
                    bend = half_s * th
                    score = half_s + bend
                    deriv = (1.0 + th) * (1.0 + half_s - bend)
                    if kb == qb:
                        score = jnp.where(lower, score, 0.0)
                        deriv = jnp.where(lower, deriv, 0.0)
                    low = score.astype(BF16)
                    spot = tile_rows(kb, qb)
                    abuf[2 * pair + hh, spot, :] = low
                    sbuf[2 * pair + hh, spot, :] = deriv.astype(BF16)
            for hh in range(2):
                for kb in range(qb + 1):
                    span = slice(kb * BLK, (kb + 1) * BLK)
                    total = total + dot(abuf[2 * pair + hh, tile_rows(kb, qb), :], vals[hh][span])
            att[qs, lanes] = total * inv_len
        return 0

    lax.fori_loop(0, H // 2, attend, 0)

    scale = 2.0 / math.sqrt(D)
    dnacc[...] = jnp.zeros_like(dnacc)
    dwo[...] = jnp.zeros_like(dwo)
    carry[...] = jnp.zeros_like(carry)
    first_row = iota((BLK, 1), 0) == 0
    last_row = iota((BLK, 1), 0) == BLK - 1

    def middle(block, sums):
        sum_loss, sum_o, sum_b, dg1, dg2 = sums
        rows = at(block)
        x = xs[rows, :]
        pos = block * BLK + iota((BLK, 1), 0)
        live = pos < length
        valid = pos < length - 1
        o = att[rows, :]
        u = gate[rows, :]
        ms_o = mean_last(o * o)
        r2 = lax.rsqrt(ms_o + EPSILON)
        n2 = o * r2 * gains_ref[1:2, :]
        g = (n2 * u).astype(BF16)
        branch = dot(g, wo_ref[...])
        ms_b = mean_last(branch * branch)
        mixed = x + branch
        r3 = lax.rsqrt(mean_last(mixed * mixed) + EPSILON)
        final = (mixed * r3 * gains_ref[2:3, :]).astype(BF16)
        final_f = final.astype(F32)
        after = xs[pl.ds(pl.multiple_of(block * BLK + BLK, 8), 8), :][0:1, :]
        nxt = jnp.where(last_row, after, pltpu.roll(x, BLK - 1, 0))
        target = jnp.sum(final_f * nxt, -1, keepdims=True) * scale
        logits = dot_nt(final, neg[...]) * scale
        top = jnp.maximum(jnp.max(logits, -1, keepdims=True), target)
        powers = jnp.exp(logits - top)
        near = jnp.exp(target - top)
        total = near + jnp.sum(powers, -1, keepdims=True)
        lse = top + jnp.log(total)
        weight = jnp.where(valid, 1.0 / total_tokens, 0.0)
        share = weight / total
        dt_ = (share * near - weight) * scale
        dz = (share * powers).astype(BF16)
        dfin = dt_ * nxt + scale * dot(dz, neg[...])
        dnacc[...] += dot_tn(dz, final)
        dnext = dt_ * final_f
        shifted = jnp.where(first_row, carry[0:1, :], pltpu.roll(dnext, 1, 0))
        carry[...] = jnp.broadcast_to(dnext[BLK - 1 : BLK, :], carry.shape)
        unit3 = mixed * r3
        dg2 = dg2 + jnp.sum(dfin * unit3, 0, keepdims=True)
        scaled = dfin * gains_ref[2:3, :]
        dy = r3 * (scaled - unit3 * mean_last(scaled * unit3))
        att[rows, :] = dy + shifted
        db = dy.astype(BF16)
        dwo[...] += dot_tn(g, db)
        dg = dot_nt(db, wo_ref[...])
        dp_ref[rows, 0:D] = (0.5 * dg * n2 * deriv_ref[rows, 0:D].astype(F32)).astype(BF16)
        dn2 = dg * u
        unit2 = o * r2
        dg1 = dg1 + jnp.sum(dn2 * unit2, 0, keepdims=True)
        scaled2 = dn2 * gains_ref[1:2, :]
        do = (r2 * (0.5 * inv_len)) * (scaled2 - unit2 * mean_last(scaled2 * unit2))
        do_ref[rows, :] = do.astype(BF16)
        return (
            sum_loss + jnp.sum(jnp.where(valid, lse - target, 0.0), keepdims=True),
            sum_o + jnp.sum(jnp.where(live, root_mean(ms_o), 0.0), keepdims=True),
            sum_b + jnp.sum(jnp.where(live, root_mean(ms_b), 0.0), keepdims=True),
            dg1,
            dg2,
        )

    zero = jnp.zeros((1, 1), F32)
    zrow = jnp.zeros((1, D), F32)
    sum_loss, sum_o, sum_b, dg1, dg2 = lax.fori_loop(0, blocks, middle, (zero, zero, zero, zrow, zrow))
    rows_ref[seq_len:requests, :] = (dnacc[...] * scale).astype(BF16)
    which = iota((8, 128), 0)
    stats = jnp.where(which == 0, sum_loss, 0.0) + jnp.where(which == 1, sum_x, 0.0)
    stats_ref[...] = stats + jnp.where(which == 2, sum_o, 0.0) + jnp.where(which == 3, sum_b, 0.0)

    ones = one_hot(iota((16, seq_len), 0) == 0)
    alive = iota((seq_len, 1), 0) < length

    def attend_back(pair, _):
        lanes = pl.ds(pl.multiple_of(pair * 128, 128), 128)
        keys = [k_ref[:, lanes] * side for side in sides]
        vals = [v_ref[:, lanes] * side for side in sides]
        grads = do_ref[:, lanes]
        qtr = q_ref[:, lanes].astype(F32).T.astype(BF16)
        dtr = grads.astype(F32).T.astype(BF16)
        for hh in range(2):
            qt[hh, 0:64, :] = qtr[hh * 64 : hh * 64 + 64, :]
            qt[hh, 64:80, :] = ones
            dt[hh] = dtr[hh * 64 : hh * 64 + 64, :]
        dql = pl.ds(pl.multiple_of(2 * D + pair * 128, 128), 128)
        for qb in range(blocks):
            qs = slice(qb * BLK, (qb + 1) * BLK)
            dq = jnp.zeros((BLK, 128), F32)
            for hh in range(2):
                for kb in range(qb + 1):
                    span = slice(kb * BLK, (kb + 1) * BLK)
                    spot = tile_rows(kb, qb)
                    slope = sbuf[2 * pair + hh, spot, :].astype(F32)
                    ds = (dot_nt(grads[qs], vals[hh][span]) * slope).astype(BF16)
                    sbuf[2 * pair + hh, spot, :] = ds
                for kb in range(qb + 1):
                    dq = dq + dot(sbuf[2 * pair + hh, tile_rows(kb, qb), :], keys[hh][kb * BLK : (kb + 1) * BLK])
            dq = dq * (0.5 * (D // H) ** -0.5)
            dp_ref[qs, dql] = (dq * deriv_ref[qs, dql].astype(F32)).astype(BF16)
        for hh in range(2):
            for kb in range(blocks):
                span = slice(kb * BLK, (kb + 1) * BLK)
                column = slice(tile_rows(kb, kb).start, tile_rows(kb, blocks - 1).stop)
                kt[hh, :, span] = dot(qt[hh, :, kb * BLK :], sbuf[2 * pair + hh, column, :])
                vt[hh, :, span] = dot(dt[hh, :, kb * BLK :], abuf[2 * pair + hh, column, :])
        dkl = pl.ds(pl.multiple_of(3 * D + pair * 128, 128), 128)
        dvl = pl.ds(pl.multiple_of(D + pair * 128, 128), 128)
        dk = jnp.concatenate([kt[0, 0:64, :], kt[1, 0:64, :]], 0).T
        dv = jnp.concatenate([vt[0], vt[1]], 0).T
        dp_ref[:, dkl] = (dk * deriv_ref[:, dkl].astype(F32)).astype(BF16)
        dp_ref[:, dvl] = (jnp.where(alive, dv, 0.0) * deriv_ref[:, dvl].astype(F32)).astype(BF16)
        for hh in range(2):
            dkb[pl.ds(2 * pair + hh, 1), :] = kt[hh, 64:65, :]
        return 0

    lax.fori_loop(0, H // 2, attend_back, 0)
    buckets = jnp.where(bucketr_ref[...] == iota((NB, seq_len), 0), 1.0, 0.0)
    dbias_ref[...] = lax.dot_general(dkb[...], buckets, NT, precision=HIGH, preferred_element_type=F32)

    def tail(block, dg0):
        rows = at(block)
        x = xs[rows, :]
        r1 = lax.rsqrt(mean_last(x * x) + EPSILON)
        unit1 = x * r1
        dn1 = dot_nt(dp_ref[rows, :], w_ref[...])
        dg0 = dg0 + jnp.sum(dn1 * unit1, 0, keepdims=True)
        scaled = dn1 * (2.0 * gains_ref[0:1, :])
        dx = r1 * (scaled - unit1 * mean_last(scaled * unit1)) + att[rows, :]
        rows_ref[rows, :] = dx.astype(BF16)
        return dg0

    dg0 = 2.0 * lax.fori_loop(0, blocks, tail, zrow)
    row = iota((8, D), 0)
    gsum = jnp.where(row == 0, dg0, 0.0) + jnp.where(row == 1, dg1, 0.0)
    dgain_ref[...] = gsum + jnp.where(row == 2, dg2, 0.0)

    copy_rows.start()

    half = keep_ref.shape[0] // BLK

    def write(block, values):
        rows = slice(block % half * BLK, (block % half + 1) * BLK)

        @pl.when(core_ref[0] == block // half)
        def _():
            keep_ref[rows, :] = values

        @pl.when(core_ref[0] != block // half)
        def _():
            give_ref[rows, :] = values

    for side in range(D // BLK):
        rows = slice(side * BLK, (side + 1) * BLK)
        write(side, dwo[rows, :].astype(BF16))
        turned = n1_ref[:, rows].astype(F32).T.astype(BF16)
        for part in range(4):
            grad = dot(turned, dp_ref[:, part * D : (part + 1) * D])
            write((part + 1) * (D // BLK) + side, grad.astype(BF16))
    copy_rows.wait()


def step(length, core, own, far, slotc, w, wo, gains, time_bias, buckets, total_tokens):
    seq_len = buckets.shape[1]
    requests = slotc.shape[0]
    negs = requests - seq_len
    hbm = pl.BlockSpec(memory_space=pl.ANY)
    vmem = pl.BlockSpec(memory_space=pltpu.VMEM)
    blocks = seq_len // BLK
    tiles = blocks * (blocks + 1) // 2
    outs = (
        sds(requests, D),
        sds(5 * D // 2, D),
        sds(5 * D // 2, D),
        sds(H, NB, dtype=F32),
        sds(8, 128, dtype=F32),
        sds(8, D, dtype=F32),
    )
    return pl.pallas_call(
        functools.partial(step_kernel, total_tokens),
        out_shape=outs,
        in_specs=[pl.BlockSpec(memory_space=pltpu.SMEM)] * 2 + [vmem] * 3 + [hbm] * 2 + [vmem] * 4,
        out_specs=[hbm] + [vmem] * (len(outs) - 1),
        scratch_shapes=[
            pltpu.VMEM((seq_len, D), BF16),
            pltpu.VMEM((seq_len, 4 * D), BF16),
            pltpu.VMEM((seq_len + 8, D), F32),
            pltpu.VMEM((negs, D), BF16),
            pltpu.VMEM((seq_len, D), F32),
            pltpu.VMEM((seq_len, 4 * D), BF16),
            pltpu.VMEM((seq_len, D), F32),
            pltpu.VMEM((seq_len, D), BF16),
            pltpu.VMEM((seq_len, D), BF16),
            pltpu.VMEM((seq_len, D), BF16),
            pltpu.VMEM((seq_len, D), BF16),
            pltpu.VMEM((seq_len, D), BF16),
            pltpu.VMEM((H, tiles * BLK, BLK), BF16),
            pltpu.VMEM((H, tiles * BLK, BLK), BF16),
            pltpu.VMEM((negs, D), F32),
            pltpu.VMEM((D, D), F32),
            pltpu.VMEM((8, D), F32),
            pltpu.VMEM((2, 80, seq_len), BF16),
            pltpu.VMEM((2, 64, seq_len), BF16),
            pltpu.VMEM((2, 80, seq_len), F32),
            pltpu.VMEM((2, 64, seq_len), F32),
            pltpu.VMEM((H, seq_len), F32),
            pltpu.VMEM(w.shape, BF16),
            pltpu.VMEM(wo.shape, BF16),
            pltpu.VMEM((requests, D), BF16),
            pltpu.SemaphoreType.DMA((3,)),
        ],
        compiler_params=BIG_PARAMS,
        cost_estimate=pl.CostEstimate(flops=50_000_000_000, bytes_accessed=15_000_000, transcendentals=0),
        name="step",
    )(length, core, own, far, slotc, w, wo, gains, time_bias, buckets, buckets.reshape(seq_len, 1))


def spread_kernel(slotr_ref, rows_ref, far_ref, own_ref):
    slots = far_ref.shape[0]

    def put(block, _):
        slot = block * BLK + iota((BLK, 1), 0)
        far_ref[at(block), :] = dot(one_hot(slotr_ref[...] - slots == slot), rows_ref[...]).astype(BF16)
        own_ref[at(block), :] = dot(one_hot(slotr_ref[...] == slot), rows_ref[...]).astype(BF16)
        return 0

    lax.fori_loop(0, slots // BLK, put, 0)


def spread(slotr, rows, slots):
    return pl.pallas_call(
        spread_kernel,
        out_shape=(sds(slots, D), sds(slots, D)),
        compiler_params=PARAMS,
        cost_estimate=pl.CostEstimate(flops=5_000_000_000, bytes_accessed=6_000_000, transcendentals=0),
        name="spread",
    )(slotr, rows)


def gather_kernel(ids_ref, got_ref, out_ref):
    rows, slots = (out_ref.shape[0], got_ref.shape[0])
    hits = one_hot(ids_ref[...] == iota((rows, slots), 0))
    out_ref[...] = dot(hits, got_ref[...]).astype(BF16)


def row_sums(ids, got, rows):
    return pl.pallas_call(
        gather_kernel,
        out_shape=sds(rows, got.shape[1]),
        compiler_params=PARAMS,
        name="row_sums",
    )(ids, got)


def update_kernel(ids_ref, got_ref, far_ref, table_ref, acc_ref, table_out, acc_out):
    rows, slots = (table_ref.shape[0], got_ref.shape[0])
    hits = one_hot(ids_ref[...] == iota((rows, slots), 0))
    sums = dot(hits, got_ref[...]) + far_ref[...].astype(F32)
    acc = acc_ref[...] + mean_last(sums * sums)
    acc_out[...] = acc
    table_out[...] = table_ref[...] - ROW_RATE * sums * lax.rsqrt(acc)


def update_rows(ids, got, far, table, row_acc):
    rows = table.shape[0]
    new_table, new_acc = pl.pallas_call(
        update_kernel,
        out_shape=(sds(*table.shape, dtype=F32), sds(rows, 1, dtype=F32)),
        compiler_params=PARAMS,
        name="update_rows",
    )(ids, got, far, table, row_acc.reshape(rows, 1))
    return new_table, new_acc.reshape(rows)


def pick(array, index, dim):
    return lax.dynamic_index_in_dim(array, index, dim, keepdims=False)


def swap(values, axis):
    return lax.ppermute(values, axis, SWAP)


def add(left, right):
    return (left.astype(F32) + right.astype(F32)).astype(BF16)


def turn(values, axes, stage):
    pairs = []
    for place in range(8):
        core = place & 1
        flip = 4 if core == stage else 2
        pairs.append((place, place ^ flip))
    return lax.ppermute(values, axes, pairs)


def sum_chips(keep, got, order, pair):
    rows, width = keep.shape
    one = lax.axis_index(pair) == 0
    here, there = (lax.axis_index(order[0]), lax.axis_index(order[1]))
    outer = jnp.where(one, here, there)
    inner = jnp.where(one, there, here)
    plane = order[:2] + (pair,)
    terms = [values.reshape(2, 2, rows // 4, width) for values in (keep, got)]
    got = turn(add(*[pick(v, 1 - outer, 0) for v in terms]), plane, 0)
    terms = [add(*[pick(v, outer, 0) for v in terms]), got]
    got = turn(add(*[pick(v, 1 - inner, 0) for v in terms]), plane, 1)
    part = add(add(*[pick(v, inner, 0) for v in terms]), got)
    for axis in order[2:]:
        part = part.reshape(2, part.shape[0] // 2, width)
        here = lax.axis_index(axis)
        got = swap(pick(part, 1 - here, 0), axis)
        part = add(pick(part, here, 0), got)
    return part


def join(values, got, first):
    return jnp.stack([jnp.where(first, values, got), jnp.where(first, got, values)])


def share_chips(part, extra, order, pair):
    rows, width = part.shape
    packed = jnp.concatenate([part, extra], 0)
    for axis in reversed(order[2:]):
        packed = join(packed, swap(packed, axis), lax.axis_index(axis) == 0)
    one = lax.axis_index(pair) == 0
    here, there = (lax.axis_index(order[0]), lax.axis_index(order[1]))
    plane = order[:2] + (pair,)
    packed = packed.reshape(-1, rows + extra.shape[0], width)
    inner, outer = (jnp.where(one, there, here), jnp.where(one, here, there))
    packed = join(packed, turn(packed, plane, 1), inner == 0)
    packed = join(packed, turn(packed, plane, 0), outer == 0)
    whole = packed.reshape(-1, rows + extra.shape[0], width)
    return whole[:, :rows].reshape(-1, width), whole[:, rows:]


def adam_kernel(core_ref, mine_ref, other_ref, *refs):
    sources, targets, inside_, outside, sem_in, sem_out = (refs[:6], refs[6:12], refs[12:18], refs[18:24], *refs[24:])
    chunks = sem_in.shape[0]
    size = D // chunks
    half = mine_ref.shape[0] // size
    parts = 1 + sources[0].shape[1] // D

    def copy(chunk, k, incoming):
        rows = pl.ds(pl.multiple_of(chunk * size, size), size)
        if incoming:
            return pltpu.make_async_copy(sources[k].at[rows], inside_[k].at[rows], sem_in.at[chunk, k])
        return pltpu.make_async_copy(outside[k].at[rows], targets[k].at[rows], sem_out.at[chunk, k])

    def begin(chunk, _):
        for k in range(6):
            copy(chunk, k, True).start()
        return 0

    lax.fori_loop(0, chunks, begin, 0)

    def compute(chunk, _):
        for k in range(6):
            copy(chunk, k, True).wait()
        rows = pl.ds(pl.multiple_of(chunk * size, size), size)
        for part in range(parts):
            spot = part * chunks + chunk
            from_ = pl.ds(pl.multiple_of(lax.rem(spot, half) * size, size), size)
            own = spot // half == core_ref[0]
            grad = jnp.where(own, mine_ref[from_, :].astype(F32), other_ref[from_, :].astype(F32))
            first = 0 if part else 3
            columns = slice((part - 1) * D, part * D) if part else slice(None)
            w, m, v = (inside_[first + k][rows, columns] for k in range(3))
            for k, value in enumerate(adam_update(w, grad, m, v, WEIGHT_DECAY)):
                outside[first + k][rows, columns] = value
        for k in range(6):
            copy(chunk, k, False).start()
        return 0

    lax.fori_loop(0, chunks, compute, 0)

    def finish(chunk, _):
        for k in range(6):
            copy(chunk, k, False).wait()
        return 0

    lax.fori_loop(0, chunks, finish, 0)


def adam(core, mine, other, uvqk, out):
    chunks = 8
    vmem = pl.BlockSpec(memory_space=pltpu.VMEM)
    hbm = pl.BlockSpec(memory_space=pl.ANY)
    shapes = [uvqk[0].shape] * 3 + [out[0].shape] * 3
    buffers = [pltpu.VMEM(shape, F32) for shape in shapes]
    return pl.pallas_call(
        adam_kernel,
        out_shape=[sds(*shape, dtype=F32) for shape in shapes],
        in_specs=[pl.BlockSpec(memory_space=pltpu.SMEM), vmem, vmem] + [hbm] * 6,
        out_specs=[hbm] * 6,
        scratch_shapes=buffers
        + buffers
        + [pltpu.SemaphoreType.DMA((chunks, 6)), pltpu.SemaphoreType.DMA((chunks, 6))],
        compiler_params=BIG_PARAMS,
        name="adam",
    )(core, mine, other, *uvqk, *out)


def per_device(
    axes,
    table,
    row_acc,
    uvqk_weight,
    out_weight,
    time_bias,
    gains,
    uvqk_m,
    uvqk_v,
    out_m,
    out_v,
    bias_m,
    bias_v,
    gain_m,
    gain_v,
    lengths,
    time_buckets,
    item_rows,
    row_owner,
):
    every = axes
    near = axes[1:]
    devices = lax.axis_size(every)
    peers = devices // 2
    requests = item_rows.shape[0]
    capacity = max(2, 2 * requests // devices)
    rows = table.shape[0]
    slots = peers * capacity
    total_tokens = float(time_buckets.size * devices)
    half = lax.axis_index(axes[0]).reshape(1)
    core = lax.axis_index(axes[-1]).reshape(1)

    def exchange(values):
        return lax.all_to_all(values.reshape(peers, capacity, D), near, 0, 0, tiled=True).reshape(slots, D)

    table_low = table.astype(BF16)
    slotc, slotr, ids = request_slots(half, row_owner, item_rows, devices, capacity)
    ids = lax.all_to_all(ids, near, 0, 0, tiled=True)
    ids_own = ids[:, 0, :capacity]
    ids_far = ids[:, 0, capacity:]
    outer = lax.ppermute(table_low, axes[:2], [(0, 2), (3, 1)])
    inner = lax.ppermute(table_low, axes[:2], [(1, 3), (2, 0)])
    serve_own = serve(ids, [table_low], 0)
    got_own = exchange(serve_own)
    serve_far = serve(ids, [outer, inner], capacity)
    got_far = exchange(serve_far)
    own = place(slotc, got_own)

    w_low = (0.5 * uvqk_weight).astype(BF16)
    wo_low = out_weight.astype(BF16)
    row_grads, keep, give, dbias, stats, dgain = step(
        lengths, core, own, got_far, slotc, w_low, wo_low, gains, time_bias, time_buckets, total_tokens
    )
    send_far, send_own = spread(slotr, row_grads, slots)
    back_far = exchange(send_far)
    got = swap(give, axes[-1])
    order = axes[-3:-1] + axes[-4::-1]
    unit = 8 << len(order)
    pad = -keep.shape[0] % unit
    part = sum_chips(*[jnp.pad(v, ((0, pad), (0, 0))) for v in (keep, got)], order, axes[-1])
    sums_far = row_sums(ids_far.reshape(1, slots), back_far, rows)
    sums_far = lax.ppermute(sums_far, axes[0], SWAP)
    back_own = exchange(send_own)
    new_table, new_acc = update_rows(ids_own.reshape(1, slots), back_own, sums_far, table, row_acc)

    small = jnp.concatenate(
        [
            dbias.reshape(-1),
            dgain[:3].reshape(-1),
            stats[:4, 0],
            jnp.zeros((2048 - H * NB - 3 * D - 4,), F32),
        ]
    ).reshape(4, D)
    small = small + lax.ppermute(small, axes[-1], SWAP)
    small_hi = lax.reduce_precision(small, 8, 7)
    small_lo = (small - small_hi).astype(BF16)
    small_hi = small_hi.astype(BF16)
    mine, small = share_chips(part, jnp.concatenate([small_hi, small_lo], 0), order, axes[-1])
    mine = mine[: keep.shape[0]]
    other = swap(mine, axes[-1])
    small = jnp.sum(small.astype(F32), 0)
    small = (small[:4] + small[4:]).reshape(-1)
    sum_bias = small[: H * NB].reshape(H, NB)
    sum_gains = small[H * NB : H * NB + 3 * D].reshape(3, D)
    sums = small[H * NB + 3 * D : H * NB + 3 * D + 4] / total_tokens
    summary = jnp.stack([sums[0], sums[1], sums[3]])
    attention_rms = sums[2:3]

    uvqk_step, uvqk_m_new, uvqk_v_new, out_step, out_m_new, out_v_new = adam(
        core, mine, other, (uvqk_weight, uvqk_m, uvqk_v), (out_weight, out_m, out_v)
    )
    bias_step, bias_m_new, bias_v_new = adam_update(time_bias, sum_bias, bias_m, bias_v, 0.0)
    gain_step, gain_m_new, gain_v_new = adam_update(gains, sum_gains, gain_m, gain_v, 0.0)
    return (
        new_table,
        new_acc,
        uvqk_step,
        uvqk_m_new,
        uvqk_v_new,
        out_step,
        out_m_new,
        out_v_new,
        bias_step,
        bias_m_new,
        bias_v_new,
        gain_step,
        gain_m_new,
        gain_v_new,
        summary,
        attention_rms,
    )


def solution(mesh):
    sizes = (mesh.shape["dp"], mesh.shape["mp"])
    bits = [size.bit_length() - 1 for size in sizes]
    axes = tuple(f"d{i}" for i in range(bits[0])) + tuple(f"m{i}" for i in range(bits[1]))
    fine = Mesh(mesh.devices.reshape((2,) * len(axes)), axes)
    split = P(axes)
    whole = P()

    def body(*args):
        return per_device(axes, *args)

    return jax.shard_map(
        body,
        mesh=fine,
        in_specs=(split, split) + (whole,) * 12 + (split,) * 4,
        out_specs=(split, split) + (whole,) * 14,
        check_vma=False,
    )
```
